512 devices in a mesh: pix: 128 (over x, z, core), frm: 4 (over y).
Axes of the slice: x: 4, y: 4, z: 16, core: 2. Of those that a mesh axis runs over, the one named last changes fastest.
Arguments:
- frames_y: bfloat16 [16384, 2048], P('pix', 'frm'), may hold values from -6 to 6
- traces: bfloat16 [1024, 2048], P('pix', 'frm'), may hold values from -0.13183594 to 0.13183594
- footprints: float32 [16384, 1024], P('pix'), may hold values from 0 to 2
- order: int32 [1024], replicated, may hold values from 0 to 1023, each once
- support: int32 [128, 256], P('pix'), may hold values from 0 to 1023, as said below
Outputs:
- footprints_new: float32 [16384, 1024], P('pix')
The draws below stay inside these ranges and needn't reach their ends.
Inputs may be any that keep to these rules, and one draw needn't show every extreme that they name: `support`: row j lists 256 different neurons; it governs pixels j * 128 to (j + 1) * 128 - 1.
All inputs are finite; a program needn't handle non-finite values.
Results may differ from the reference program's by a relative error of at most 0.0003.
Values may be sent and summed in bfloat16 or wider, within the bound.
A program may use at most 64 MiB of HBM per device.

```python
import jax
import jax.numpy as jnp
from jax import lax

K = 1024
BLK = 128
SWEEPS = 3
SUPPORT = 256
PIX_DEV = 128
PIXELS = 16384
FRAMES = 2048
PIX_BLOCKS = 128


def draw_support(key, part):

    def one_row(row):
        listed = jax.random.permutation(jax.random.fold_in(jax.random.fold_in(key, 7301), row), K)
        return listed[:SUPPORT].astype(jnp.int32)
    return jax.vmap(one_row)(jnp.arange(PIX_BLOCKS, dtype=jnp.int32))


def levels(stream_key, extent, split, smallest, high):
    loudness = 1.0
    for dim, parts in split:
        heights = jax.random.uniform(jax.random.fold_in(jax.random.fold_in(stream_key, 6), dim), (parts,), jnp.float32, smallest / len(split), high / len(split))
        loudness = loudness * jnp.repeat(jnp.exp(heights), extent[dim] // parts).reshape((-1,) + (1,) * (len(extent) - 1 - dim))
    return loudness


def gaussian(own_key, shape, scale, bound, split=(), kind=jnp.bfloat16):
    array = scale * jax.random.normal(own_key, shape, jnp.float32)
    if split:
        array = array * levels(own_key, shape, split, -0.22, 0.18)
    return jnp.clip(array, -bound, bound).astype(kind)


def setup_inputs(seed: int = 0) -> dict:
    key_of = jax.random.split(jax.random.key(seed), 6)
    frames_y = gaussian(key_of[0], (PIXELS, FRAMES), 1.0, 6.0, ((0, 128), (1, 4)))
    traces = gaussian(key_of[1], (K, FRAMES), (FRAMES ** -0.5), 0.13183594, ((0, 128), (1, 4)))
    footprints = jnp.clip(2.0 * jax.random.uniform(key_of[2], (PIXELS, K), jnp.float32) ** levels(key_of[2], (PIXELS, K), ((0, 128),), -0.2, 0.2), 0.0, 2.0)
    order = jax.random.permutation(key_of[3], K).astype(jnp.int32)
    support = draw_support(jax.random.fold_in(key_of[5], 71), 0)
    return dict(frames_y=frames_y, traces=traces, footprints=footprints, order=order, support=support)


def reference(frames_y, traces, footprints, order, support):
    highest = lax.Precision.HIGHEST
    traces32 = traces.astype(jnp.float32)
    gram = jnp.dot(traces32, traces32.T, precision=highest)
    cross = jnp.dot(frames_y.astype(jnp.float32), traces32.T, precision=highest)
    neuron_ids = jnp.arange(K, dtype=jnp.int32)
    member = jnp.any(support[:, :, None] == neuron_ids[None, None, :], axis=1).astype(jnp.float32)
    keep = jnp.repeat(member, PIX_DEV, axis=0)
    current = jnp.take(footprints, order, axis=1)
    cross_perm = jnp.take(cross, order, axis=1)
    gram_perm = jnp.take(jnp.take(gram, order, axis=0), order, axis=1)
    keep_perm = jnp.take(keep, order, axis=1)
    diagonal = jnp.diagonal(gram_perm)
    for sweep_index in range(SWEEPS):
        for block_index in range(K // BLK):
            lower = block_index * BLK
            upper = lower + BLK
            numer = cross_perm[:, lower:upper] - jnp.dot(current, gram_perm[:, lower:upper], precision=highest)
            update = keep_perm[:, lower:upper] * jnp.maximum(current[:, lower:upper] + numer / diagonal[lower:upper], 0.0)
            scale = jnp.sqrt(lax.optimization_barrier(jnp.mean(update * update, axis=0)) + 1e-06)
            current = current.at[:, lower:upper].set(update / scale)
    return jnp.zeros_like(current).at[:, order].set(current)
```

```python
import functools

import jax
import jax.numpy as jnp
from jax import lax
from jax.experimental import pallas as pl
from jax.experimental.pallas import tpu as pltpu
from jax.sharding import PartitionSpec as P

BLK = 128
SWEEPS = 3
DIMS = (4, 4, 16, 2)
MESH = pl.DeviceIdType.MESH
F32, BF16 = jnp.float32, jnp.bfloat16


def ring_far(d, n):
    return min(d, n - d)


def plane_offsets(nx, ny, nc):
    every = [
        (dx, dy, dc)
        for dx in range(nx)
        for dy in range(ny)
        for dc in range(nc)
        if (dx, dy, dc) != (0, 0, 0)
    ]
    return sorted(every, key=lambda o: -(ring_far(o[0], nx) + ring_far(o[1], ny) + 0.1 * o[2]))


def split2(v):
    hi = v.astype(BF16)
    return hi, (v - hi.astype(F32)).astype(BF16)


def split2_xla(v):
    hi = lax.reduce_precision(v, 8, 7)
    return hi.astype(BF16), (v - hi).astype(BF16)


def dot(a, b):
    return lax.dot_general(a, b, (((1,), (0,)), ((), ())), preferred_element_type=F32)


def dot3(ahi, alo, bhi, blo):
    return dot(ahi, bhi) + (dot(ahi, blo) + dot(alo, bhi))


def hals_kernel(
    dims, blocks, pixels,
    bases, mhi, mlo, out,
    planes, slots, part, scales, acc, upd, chi, clo, oupd, ohi, olo,
    base_sem, base_send, sum_sem, sum_send, scale_sem, scale_send,
):
    nx, ny, nz, nc = dims
    group = nz // ny
    rows = out.shape[0]
    steps = SWEEPS * blocks
    devices = nx * ny * nc
    pix, y = lax.axis_index("pix"), lax.axis_index("frm")
    x, z, c = pix // (nz * nc), (pix // nc) % nz, pix % nc
    me = (x * ny + y) * nc + c
    on_plane = z == 0
    offsets = plane_offsets(nx, ny, nc)

    def place(ax, ay, az, ac):
        return ((ax * nz + az) * nc + ac, ay)

    def peer(offset):
        return place((x + offset[0]) % nx, (y + offset[1]) % ny, 0, (c + offset[2]) % nc)

    barrier = pltpu.get_barrier_semaphore()

    @pl.when(on_plane)
    def _():
        for far in range(1, nz):
            pl.semaphore_signal(barrier, inc=1, device_id=place(x, y, far, c), device_id_type=MESH)
        for offset in offsets:
            pl.semaphore_signal(barrier, inc=1, device_id=peer(offset), device_id_type=MESH)
        pl.semaphore_wait(barrier, nz - 1 + devices - 1)

    @pl.when(z != 0)
    def _():
        pl.semaphore_signal(barrier, inc=1, device_id=place(x, y, 0, c), device_id_type=MESH)
        pl.semaphore_wait(barrier, 1)

    def base_copy(i):
        return pltpu.make_async_remote_copy(
            src_ref=bases.at[i], dst_ref=planes.at[i, z // ny],
            send_sem=base_send, recv_sem=base_sem.at[i],
            device_id=place(x, y, 0, c), device_id_type=MESH,
        )

    sends_base = jnp.logical_and(z % ny == y, z != 0)
    keeps_base = jnp.logical_and(y == 0, on_plane)

    @pl.when(sends_base)
    def _():
        for i in range(2 * blocks):
            base_copy(i).start()

    @pl.when(keeps_base)
    def _():
        for i in range(2 * blocks):
            pltpu.make_async_copy(bases.at[i], planes.at[i, 0], base_sem.at[i]).start()

    def lanes(b):
        return pl.ds(pl.multiple_of(b * BLK, BLK), BLK)

    def base_index(t):
        return jnp.where(t < blocks, t, blocks + t % blocks)

    def sum_copy(t, offset):
        return pltpu.make_async_remote_copy(
            src_ref=part.at[t], dst_ref=slots.at[t, me],
            send_sem=sum_send.at[t], recv_sem=sum_sem.at[t],
            device_id=peer(offset), device_id_type=MESH,
        )

    def scale_copy(t, far):
        return pltpu.make_async_remote_copy(
            src_ref=scales.at[t], dst_ref=scales.at[t],
            send_sem=scale_send.at[t], recv_sem=scale_sem.at[t],
            device_id=place(x, y, far, c), device_id_type=MESH,
        )

    oupd[...] = jnp.maximum(bases[0], 0.0)
    ohi[...] = jnp.zeros_like(ohi)
    olo[...] = jnp.zeros_like(olo)

    def replay(t):
        b = t % blocks
        now = oupd[...] * scales[t]
        out[:, lanes(b)] = now
        hi, lo = split2(now)
        ohi[:, lanes(b)] = hi
        olo[:, lanes(b)] = lo

        @pl.when(t < steps - 1)
        def _():
            nxt = (t + 1) % blocks
            value = bases[base_index(t + 1)] - dot3(ohi[...], olo[...], mhi[nxt], mlo[nxt])
            oupd[...] = jnp.maximum(value, 0.0)

    def emit(t):
        new = jnp.maximum(acc[...], 0.0)
        upd[...] = new
        total = jnp.sum(new * new, axis=0, keepdims=True)
        part[t] = total
        slots[t, me] = total
        for offset in offsets:
            sum_copy(t, offset).start()

    def prepare(t):
        @pl.when(t < 2 * blocks)
        def _():
            pltpu.make_async_copy(planes.at[t], planes.at[t], base_sem.at[t]).wait()
        return planes[base_index(t)].reshape(group * rows, BLK)

    def receive(t):
        waited = slots.at[t, pl.ds(0, devices - 1)]
        pltpu.make_async_copy(waited, waited, sum_sem.at[t]).wait()
        squares = jnp.sum(slots[t], axis=0)
        inverse = 1.0 / jnp.sqrt(squares / pixels + 1e-06)
        scales[t] = inverse
        return inverse

    def ahead(t):
        b = t % blocks
        nxt = (t + 1) % blocks
        chi[:, lanes(b)] = jnp.zeros((group * rows, BLK), BF16)
        clo[:, lanes(b)] = jnp.zeros((group * rows, BLK), BF16)
        base = prepare(t + 1)
        acc[...] = base - dot3(chi[...], clo[...], mhi[nxt], mlo[nxt])

    def share(t):
        for far in range(nz - 1, 0, -1):
            scale_copy(t, far).start()
        replay(t)

    @pl.when(on_plane)
    def _():
        chi[...] = jnp.zeros_like(chi)
        clo[...] = jnp.zeros_like(clo)
        acc[...] = prepare(0)
        emit(0)
        ahead(0)

        @pl.loop(1, steps)
        def _(t):
            prev, b = (t - 1) % blocks, t % blocks
            now = upd[...] * receive(t - 1)
            hi, lo = split2(now)
            inner = pl.ds(pl.multiple_of(prev * BLK, BLK), BLK)
            acc[...] = acc[...] - dot3(hi, lo, mhi[b, inner], mlo[b, inner])
            emit(t)
            chi[:, lanes(prev)] = hi
            clo[:, lanes(prev)] = lo
            share(t - 1)

            @pl.when(t < steps - 1)
            def _():
                ahead(t)

        receive(steps - 1)
        share(steps - 1)

        @pl.loop(0, steps)
        def _(t):
            for offset in offsets:
                sum_copy(t, offset).wait_send()
            for far in range(nz - 1, 0, -1):
                scale_copy(t, far).wait_send()

    @pl.when(z != 0)
    def _():
        @pl.loop(0, steps)
        def _(t):
            pltpu.make_async_copy(scales.at[t], scales.at[t], scale_sem.at[t]).wait()
            replay(t)

    @pl.when(sends_base)
    def _():
        for i in range(2 * blocks):
            base_copy(i).wait_send()


def hals(dims, bases, mhi, mlo, rows, pixels):
    nx, ny, nz, nc = dims
    neurons = mhi.shape[1]
    blocks = neurons // BLK
    steps = SWEEPS * blocks
    group = nz // ny
    devices = nx * ny * nc
    dma = pltpu.SemaphoreType.DMA
    return pl.pallas_call(
        functools.partial(hals_kernel, dims, blocks, pixels),
        out_shape=jax.ShapeDtypeStruct((rows, neurons), F32),
        in_specs=[pl.BlockSpec(memory_space=pltpu.VMEM)] * 3,
        out_specs=pl.BlockSpec(memory_space=pltpu.VMEM),
        scratch_shapes=[
            pltpu.VMEM((2 * blocks, group, rows, BLK), F32),
            pltpu.VMEM((steps, devices, 1, BLK), F32),
            pltpu.VMEM((steps, 1, BLK), F32),
            pltpu.VMEM((steps, 1, BLK), F32),
            pltpu.VMEM((group * rows, BLK), F32),
            pltpu.VMEM((group * rows, BLK), F32),
            pltpu.VMEM((group * rows, neurons), BF16),
            pltpu.VMEM((group * rows, neurons), BF16),
            pltpu.VMEM((rows, BLK), F32),
            pltpu.VMEM((rows, neurons), BF16),
            pltpu.VMEM((rows, neurons), BF16),
            dma((2 * blocks,)),
            dma,
            dma((steps,)),
            dma((steps,)),
            dma((steps,)),
            dma((steps,)),
        ],
        compiler_params=pltpu.CompilerParams(collective_id=1, has_side_effects=True),
        name="hals",
    )(bases, mhi, mlo)


def local(dims, frames_y, traces, footprints, order, support):
    highest = lax.Precision.HIGHEST
    rows = frames_y.shape[0]
    neurons = footprints.shape[1]
    blocks = neurons // BLK
    pixels = rows * lax.axis_size("pix")
    ids = lax.iota(jnp.int32, neurons)
    contract = (((1,), (1,)), ((), ()))

    wide = lax.all_gather(frames_y, "frm", axis=1, tiled=True)
    every = lax.all_gather(traces, "pix", axis=0, tiled=True)
    every = lax.all_gather(every, "frm", axis=1, tiled=True)

    onehot = order[:, None] == ids[None, :]
    sorted_traces = dot(onehot.astype(BF16), every).astype(BF16)
    own = jnp.dot(footprints, onehot.astype(F32).T, precision=highest)
    listed = jnp.any(support[0][:, None] == order[None, :], axis=0)

    gram = lax.dot_general(sorted_traces, sorted_traces, contract, preferred_element_type=F32)
    cross = lax.dot_general(wide, sorted_traces, contract, preferred_element_type=F32)
    wide_traces = sorted_traces.astype(F32)
    diagonal = jnp.sum(wide_traces * wide_traces, axis=1)
    ratio = jnp.where(ids[:, None] == ids[None, :], 0.0, gram) / diagonal[None, :]
    ratio = ratio.reshape(neurons, blocks, BLK).swapaxes(0, 1)
    mhi, mlo = split2_xla(ratio)

    later = (ids // BLK)[None, :, None] >= jnp.arange(blocks)[:, None, None]
    zero = jnp.zeros((), BF16)
    owhi, owlo = split2_xla(own)
    mhi_later, mlo_later = jnp.where(later, mhi, zero), jnp.where(later, mlo, zero)
    batch = lambda a, b: jnp.einsum("pk,bkj->bpj", a, b, preferred_element_type=F32)
    old = batch(owhi, mhi_later) + (batch(owhi, mlo_later) + batch(owlo, mhi_later))
    start = (cross / diagonal[None, :]).reshape(rows, blocks, BLK).swapaxes(0, 1)
    bases = jnp.concatenate([start - old, start], axis=0)
    kept = jnp.tile(listed.reshape(blocks, 1, BLK), (2, 1, 1))
    bases = jnp.where(kept, bases, -jnp.inf)

    current = hals(dims, bases, mhi, mlo, rows, pixels)
    return jnp.dot(current, onehot.astype(F32), precision=highest)


def solution(mesh, dims=DIMS):
    placed = (P("pix", "frm"), P("pix", "frm"), P("pix", None), P(), P("pix", None))
    return jax.shard_map(
        functools.partial(local, dims), mesh=mesh, in_specs=placed,
        out_specs=P("pix", None), check_vma=False,
    )
```

```python
import functools

import jax
import jax.numpy as jnp
from jax import lax
from jax.experimental import pallas as pl
from jax.experimental.pallas import tpu as pltpu
from jax.sharding import PartitionSpec as P

BLK = 128
SWEEPS = 3
DIMS = (4, 4, 16, 2)
MESH = pl.DeviceIdType.MESH
F32, BF16 = jnp.float32, jnp.bfloat16


def ring_far(d, n):
    return min(d, n - d)


def plane_offsets(nx, ny, nc):
    every = [
        (dx, dy, dc)
        for dx in range(nx)
        for dy in range(ny)
        for dc in range(nc)
        if (dx, dy, dc) != (0, 0, 0)
    ]
    return sorted(every, key=lambda o: -(ring_far(o[0], nx) + ring_far(o[1], ny) + 0.1 * o[2]))


def split2(v):
    hi = v.astype(BF16)
    return hi, (v - hi.astype(F32)).astype(BF16)


def dot(a, b):
    return lax.dot_general(a, b, (((1,), (0,)), ((), ())), preferred_element_type=F32)


def dot3(ahi, alo, bhi, blo):
    return dot(ahi, bhi) + (dot(ahi, blo) + dot(alo, bhi))


def dot_t(a, b):
    return lax.dot_general(a, b, (((1,), (1,)), ((), ())), preferred_element_type=F32)


def cnmf_kernel(
    dims, pixels,
    frames, traces, footprints, onehot, kept, out,
    every, wide, ordered, fhi, flo, bases, mhi, mlo,
    own_sem, wide_sem, z_sem, first_sem, second_sem, core_sem, gather_send,
    planes, slots, sums, scales, acc, upd, chi, clo, oupd, ohi, olo,
    base_sem, base_send, sum_sem, sum_send, scale_sem, scale_send,
):
    nx, ny, nz, nc = dims
    group = nz // ny
    rows, neurons = out.shape
    blocks = neurons // BLK
    steps = SWEEPS * blocks
    devices = nx * ny * nc
    half = nz // 2
    slab, span = traces.shape
    pix, y = lax.axis_index("pix"), lax.axis_index("frm")
    x, z, c = pix // (nz * nc), (pix // nc) % nz, pix % nc
    me = (x * ny + y) * nc + c
    on_plane = z == 0
    offsets = plane_offsets(nx, ny, nc)

    def place(ax, ay, az, ac):
        return ((ax * nz + az) * nc + ac, ay)

    def peer(offset):
        return place((x + offset[0]) % nx, (y + offset[1]) % ny, 0, (c + offset[2]) % nc)

    barrier = pltpu.get_barrier_semaphore()

    def at_z(far):
        return place(x, y, (z + far) % nz, c)

    def at_x(far):
        return place((x + far) % nx, y, z, c)

    def at_y(far):
        return place(x, (y + far) % ny, z, c)

    other_core = place(x, y, z, (c + 1) % nc)
    near = (
        [at_z(far) for far in range(1, nz)]
        + [at_x(far) for far in range(1, nx)]
        + [at_y(far) for far in range(1, ny)]
        + [other_core] * (nc - 1)
    )
    apart = [o for o in offsets if (o[0] != 0) + (o[1] != 0) + (o[2] != 0) > 1]

    def greet(devices):
        for device in devices:
            pl.semaphore_signal(barrier, inc=1, device_id=device, device_id_type=MESH)

    greet(near)

    @pl.when(on_plane)
    def _():
        greet([peer(offset) for offset in apart])
        pl.semaphore_wait(barrier, len(near) + len(apart))

    @pl.when(z != 0)
    def _():
        pl.semaphore_wait(barrier, len(near))

    mine = pl.ds(pl.multiple_of(c * slab, slab), slab)

    def remote(src, dst, sem, device):
        return pltpu.make_async_remote_copy(
            src_ref=src, dst_ref=dst, send_sem=gather_send, recv_sem=sem,
            device_id=device, device_id_type=MESH,
        )

    def arrived(ref, sem):
        pltpu.make_async_copy(ref, ref, sem).wait()

    sent = []

    def send(*copy):
        remote(*copy).start()
        sent.append(copy)

    home = every.at[y, x * nz + z, mine]
    own = pltpu.make_async_copy(traces, home, own_sem.at[0])
    own.start()
    for far in sorted(range(1, nz), key=lambda far: -ring_far(far, nz)):
        send(traces, home, z_sem, at_z(far))
    wide_part = wide.at[:, pl.ds(pl.multiple_of(y * span, span), span)]
    own_wide = pltpu.make_async_copy(frames, wide_part, own_sem.at[1])
    own_wide.start()
    for far in range(1, ny):
        send(frames, wide_part, wide_sem, at_y(far))

    old = footprints[...]
    hi, lo = split2(old)
    fhi[...] = dot_t(hi, onehot[...]).astype(BF16)
    flo[...] = dot_t(lo, onehot[...]).astype(BF16)

    own.wait()
    own_wide.wait()

    def low(ay, ax):
        return every.at[ay, pl.ds(ax * nz, half), mine]

    def high(ay, ax):
        return every.at[ay, pl.ds(ax * nz + half, half), mine]

    arrived(every.at[y, pl.ds(0, nz - 1), mine], z_sem)
    for far in range(1, nx):
        send(low(y, x), low(y, x), first_sem.at[0, far - 1], at_x(far))
    for far in range(1, ny):
        send(high(y, x), high(y, x), first_sem.at[1, far - 1], at_y(far))

    def finish(kind, part, ref):
        if nc > 1:
            send(ref, ref, core_sem.at[kind, part], other_core)

    def pass_on(kind, part, ref):
        peers, name = (ny, at_y) if kind == 0 else (nx, at_x)
        for far in range(1, peers):
            send(ref, ref, second_sem.at[kind, far - 1, part], name(far))
        finish(kind, part, ref)

    pass_on(0, 0, low(y, x))
    pass_on(1, 0, high(y, x))
    for far in range(1, max(nx, ny)):
        if far < nx:
            ref = low(y, (x + nx - far) % nx)
            arrived(ref, first_sem.at[0, far - 1])
            pass_on(0, far, ref)
        if far < ny:
            ref = high((y + ny - far) % ny, x)
            arrived(ref, first_sem.at[1, far - 1])
            pass_on(1, far, ref)
    for part in range(max(nx, ny)):
        for far in range(1, max(nx, ny)):
            if part < nx and far < ny:
                ref = low((y + ny - far) % ny, (x + nx - part) % nx)
                arrived(ref, second_sem.at[0, far - 1, part])
                finish(0, nx * far + part, ref)
            if part < ny and far < nx:
                ref = high((y + ny - part) % ny, (x + nx - far) % nx)
                arrived(ref, second_sem.at[1, far - 1, part])
                finish(1, ny * far + part, ref)
    if nc > 1:
        for part in range(nx * ny):
            arrived(low(0, 0), core_sem.at[0, part])
            arrived(high(0, 0), core_sem.at[1, part])
    arrived(wide.at[:, pl.ds(0, (ny - 1) * span)], wide_sem)

    width = min(256, neurons)

    @pl.loop(0, ny * span // width)
    def _(q):
        block = every[q * width // span, :, :, pl.ds(pl.multiple_of(q * width % span, width), width)]
        block = block.reshape(neurons, width)
        ordered[:, pl.ds(pl.multiple_of(q * width, width), width)] = dot(onehot[...], block).astype(BF16)

    @pl.loop(0, neurons // width)
    def _(q):
        some = ordered[pl.ds(pl.multiple_of(q * width, width), width), :]
        gram = dot_t(ordered[...], some)
        row = lax.broadcasted_iota(jnp.int32, gram.shape, 0)
        column = lax.broadcasted_iota(jnp.int32, gram.shape, 1) + q * width
        same = row == column
        diagonal = jnp.sum(jnp.where(same, gram, 0.0), axis=0, keepdims=True)
        hi, lo = split2(jnp.where(same, 0.0, gram) / diagonal)
        start = dot_t(wide[...], some) / diagonal
        for i in range(width // BLK):
            part = slice(i * BLK, (i + 1) * BLK)
            b = q * (width // BLK) + i
            mhi[b] = hi[:, part]
            mlo[b] = lo[:, part]
            bases[blocks + b] = jnp.where(kept[b] > 0.0, start[:, part], -jnp.inf)

    def base_copy(i):
        return pltpu.make_async_remote_copy(
            src_ref=bases.at[i], dst_ref=planes.at[i, z // ny],
            send_sem=base_send, recv_sem=base_sem.at[i],
            device_id=place(x, y, 0, c), device_id_type=MESH,
        )

    sends_base = jnp.logical_and(z % ny == y, z != 0)
    keeps_base = jnp.logical_and(y == 0, on_plane)

    def lanes(b):
        return pl.ds(pl.multiple_of(b * BLK, BLK), BLK)

    def hand_over(i):
        @pl.when(sends_base)
        def _():
            base_copy(i).start()

        @pl.when(keeps_base)
        def _():
            pltpu.make_async_copy(bases.at[i], planes.at[i, 0], base_sem.at[i]).start()

    @pl.loop(0, blocks)
    def _(b):
        bases[b] = bases[blocks + b] - dot3(fhi[...], flo[...], mhi[b], mlo[b])
        hand_over(b)
        fhi[:, lanes(b)] = jnp.zeros((rows, BLK), BF16)
        flo[:, lanes(b)] = jnp.zeros((rows, BLK), BF16)

    @pl.loop(blocks, 2 * blocks)
    def _(b):
        hand_over(b)

    def base_index(t):
        return jnp.where(t < blocks, t, blocks + t % blocks)

    def sum_copy(t, offset):
        return pltpu.make_async_remote_copy(
            src_ref=sums.at[t], dst_ref=slots.at[t, me],
            send_sem=sum_send.at[t], recv_sem=sum_sem.at[t],
            device_id=peer(offset), device_id_type=MESH,
        )

    def scale_copy(t, far):
        return pltpu.make_async_remote_copy(
            src_ref=scales.at[t], dst_ref=scales.at[t],
            send_sem=scale_send.at[t], recv_sem=scale_sem.at[t],
            device_id=place(x, y, far, c), device_id_type=MESH,
        )

    oupd[...] = jnp.maximum(bases[0], 0.0)
    out[...] = jnp.zeros_like(out)
    ohi[...] = jnp.zeros_like(ohi)
    olo[...] = jnp.zeros_like(olo)

    def replay(t):
        b = t % blocks
        now = oupd[...] * scales[t]
        hi, lo = split2(now)
        ohi[:, lanes(b)] = hi
        olo[:, lanes(b)] = lo

        @pl.when(t >= steps - blocks)
        def _():
            rest = ((now - hi.astype(F32)) - lo.astype(F32)).astype(BF16)
            back = onehot[lanes(b), :]
            out[...] += (dot(hi, back) + dot(lo, back)) + dot(rest, back)

        @pl.when(t < steps - 1)
        def _():
            nxt = (t + 1) % blocks
            value = bases[base_index(t + 1)] - dot3(ohi[...], olo[...], mhi[nxt], mlo[nxt])
            oupd[...] = jnp.maximum(value, 0.0)

    def emit(t):
        new = jnp.maximum(acc[...], 0.0)
        upd[...] = new
        total = jnp.sum(new * new, axis=0, keepdims=True)
        sums[t] = total
        slots[t, me] = total
        for offset in offsets:
            sum_copy(t, offset).start()

    def prepare(t):
        @pl.when(t < 2 * blocks)
        def _():
            pltpu.make_async_copy(planes.at[t], planes.at[t], base_sem.at[t]).wait()
        return planes[base_index(t)].reshape(group * rows, BLK)

    def receive(t):
        waited = slots.at[t, pl.ds(0, devices - 1)]
        pltpu.make_async_copy(waited, waited, sum_sem.at[t]).wait()
        squares = jnp.sum(slots[t], axis=0)
        inverse = 1.0 / jnp.sqrt(squares / pixels + 1e-06)
        scales[t] = inverse
        return inverse

    def ahead(t):
        b = t % blocks
        nxt = (t + 1) % blocks
        chi[:, lanes(b)] = jnp.zeros((group * rows, BLK), BF16)
        clo[:, lanes(b)] = jnp.zeros((group * rows, BLK), BF16)
        base = prepare(t + 1)
        acc[...] = base - dot3(chi[...], clo[...], mhi[nxt], mlo[nxt])

    def share(t):
        for far in range(nz - 1, 0, -1):
            scale_copy(t, far).start()
        replay(t)

    @pl.when(on_plane)
    def _():
        chi[...] = jnp.zeros_like(chi)
        clo[...] = jnp.zeros_like(clo)
        acc[...] = prepare(0)
        emit(0)
        ahead(0)

        @pl.loop(1, steps)
        def _(t):
            prev, b = (t - 1) % blocks, t % blocks
            now = upd[...] * receive(t - 1)
            hi, lo = split2(now)
            inner = pl.ds(pl.multiple_of(prev * BLK, BLK), BLK)
            acc[...] = acc[...] - dot3(hi, lo, mhi[b, inner], mlo[b, inner])
            emit(t)
            chi[:, lanes(prev)] = hi
            clo[:, lanes(prev)] = lo
            share(t - 1)

            @pl.when(t < steps - 1)
            def _():
                ahead(t)

        receive(steps - 1)
        share(steps - 1)

        @pl.loop(0, steps)
        def _(t):
            for offset in offsets:
                sum_copy(t, offset).wait_send()
            for far in range(nz - 1, 0, -1):
                scale_copy(t, far).wait_send()

    @pl.when(z != 0)
    def _():
        @pl.loop(0, steps)
        def _(t):
            pltpu.make_async_copy(scales.at[t], scales.at[t], scale_sem.at[t]).wait()
            replay(t)

    @pl.when(sends_base)
    def _():
        for i in range(2 * blocks):
            base_copy(i).wait_send()

    for copy in sent:
        remote(*copy).wait_send()


def local(dims, frames_y, traces, footprints, order, support):
    nx, ny, nz, nc = dims
    rows, span = frames_y.shape
    slab = traces.shape[0]
    neurons = footprints.shape[1]
    blocks = neurons // BLK
    steps = SWEEPS * blocks
    group = nz // ny
    devices = nx * ny * nc
    pixels = rows * lax.axis_size("pix")
    ids = lax.iota(jnp.int32, neurons)
    onehot = (order[:, None] == ids[None, :]).astype(BF16)
    listed = jnp.any(support[0][:, None] == order[None, :], axis=0)
    kept = listed.astype(F32).reshape(blocks, 1, BLK)
    dma = pltpu.SemaphoreType.DMA
    most = max(nx, ny)
    return pl.pallas_call(
        functools.partial(cnmf_kernel, dims, pixels),
        out_shape=jax.ShapeDtypeStruct((rows, neurons), F32),
        in_specs=[pl.BlockSpec(memory_space=pltpu.VMEM)] * 5,
        out_specs=pl.BlockSpec(memory_space=pltpu.VMEM),
        scratch_shapes=[
            pltpu.VMEM((ny, nx * nz, nc * slab, span), BF16),
            pltpu.VMEM((rows, ny * span), BF16),
            pltpu.VMEM((neurons, ny * span), BF16),
            pltpu.VMEM((rows, neurons), BF16),
            pltpu.VMEM((rows, neurons), BF16),
            pltpu.VMEM((2 * blocks, rows, BLK), F32),
            pltpu.VMEM((blocks, neurons, BLK), BF16),
            pltpu.VMEM((blocks, neurons, BLK), BF16),
            dma((2,)),
            dma,
            dma,
            dma((2, most - 1)),
            dma((2, most - 1, most)),
            dma((2, nx * ny)),
            dma,
            pltpu.VMEM((2 * blocks, group, rows, BLK), F32),
            pltpu.VMEM((steps, devices, 1, BLK), F32),
            pltpu.VMEM((steps, 1, BLK), F32),
            pltpu.VMEM((steps, 1, BLK), F32),
            pltpu.VMEM((group * rows, BLK), F32),
            pltpu.VMEM((group * rows, BLK), F32),
            pltpu.VMEM((group * rows, neurons), BF16),
            pltpu.VMEM((group * rows, neurons), BF16),
            pltpu.VMEM((rows, BLK), F32),
            pltpu.VMEM((rows, neurons), BF16),
            pltpu.VMEM((rows, neurons), BF16),
            dma((2 * blocks,)),
            dma,
            dma((steps,)),
            dma((steps,)),
            dma((steps,)),
            dma((steps,)),
        ],
        compiler_params=pltpu.CompilerParams(collective_id=1, has_side_effects=True),
        name="cnmf",
    )(frames_y, traces, footprints, onehot, kept)


def solution(mesh, dims=DIMS):
    placed = (P("pix", "frm"), P("pix", "frm"), P("pix", None), P(), P("pix", None))
    return jax.shard_map(
        functools.partial(local, dims), mesh=mesh, in_specs=placed,
        out_specs=P("pix", None), check_vma=False,
    )
```

```python
import functools

import jax
import jax.numpy as jnp
from jax import lax
from jax.experimental import pallas as pl
from jax.experimental.pallas import tpu as pltpu
from jax.sharding import PartitionSpec as P

BLK = 128
SWEEPS = 3
DIMS = (4, 4, 16, 2)
MESH = pl.DeviceIdType.MESH
F32, BF16 = jnp.float32, jnp.bfloat16


def ring_far(d, n):
    return min(d, n - d)


def plane_offsets(nx, ny, nc):
    every = [
        (dx, dy, dc)
        for dx in range(nx)
        for dy in range(ny)
        for dc in range(nc)
        if (dx, dy, dc) != (0, 0, 0)
    ]
    return sorted(every, key=lambda o: -(ring_far(o[0], nx) + ring_far(o[1], ny) + 0.1 * o[2]))


def split2(v):
    hi = v.astype(BF16)
    return hi, (v - hi.astype(F32)).astype(BF16)


def dot(a, b):
    return lax.dot_general(a, b, (((1,), (0,)), ((), ())), preferred_element_type=F32)


def dot3(ahi, alo, bhi, blo):
    return dot(ahi, bhi) + (dot(ahi, blo) + dot(alo, bhi))


def dot_t(a, b):
    return lax.dot_general(a, b, (((1,), (1,)), ((), ())), preferred_element_type=F32)


def cnmf_kernel(
    dims, pixels,
    frames, traces, footprints, order, support, out,
    onehot, kept, every, wide, ordered, fhi, flo, bases, mhi, mlo,
    own_sem, wide_sem, z_sem, first_sem, second_sem, core_sem, gather_send,
    planes, slots, sums, scales, acc, upd, chi, clo, oupd, ohi, olo,
    base_sem, base_send, sum_sem, sum_send, scale_sem, scale_send,
):
    nx, ny, nz, nc = dims
    group = nz // ny
    rows, neurons = out.shape
    blocks = neurons // BLK
    steps = SWEEPS * blocks
    devices = nx * ny * nc
    half = nz // 2
    slab, span = traces.shape
    pix, y = lax.axis_index("pix"), lax.axis_index("frm")
    x, z, c = pix // (nz * nc), (pix // nc) % nz, pix % nc
    me = (x * ny + y) * nc + c
    on_plane = z == 0
    offsets = plane_offsets(nx, ny, nc)

    def place(ax, ay, az, ac):
        return ((ax * nz + az) * nc + ac, ay)

    def peer(offset):
        return place((x + offset[0]) % nx, (y + offset[1]) % ny, 0, (c + offset[2]) % nc)

    barrier = pltpu.get_barrier_semaphore()

    def at_z(far):
        return place(x, y, (z + far) % nz, c)

    def at_x(far):
        return place((x + far) % nx, y, z, c)

    def at_y(far):
        return place(x, (y + far) % ny, z, c)

    other_core = place(x, y, z, (c + 1) % nc)
    near = (
        [at_z(far) for far in range(1, nz)]
        + [at_x(far) for far in range(1, nx)]
        + [at_y(far) for far in range(1, ny)]
        + [other_core] * (nc - 1)
    )
    apart = [o for o in offsets if (o[0] != 0) + (o[1] != 0) + (o[2] != 0) > 1]

    def greet(devices):
        for device in devices:
            pl.semaphore_signal(barrier, inc=1, device_id=device, device_id_type=MESH)

    greet(near)

    @pl.when(on_plane)
    def _():
        greet([peer(offset) for offset in apart])
        pl.semaphore_wait(barrier, len(near) + len(apart))

    @pl.when(z != 0)
    def _():
        pl.semaphore_wait(barrier, len(near))

    mine = pl.ds(pl.multiple_of(c * slab, slab), slab)

    def remote(src, dst, sem, device):
        return pltpu.make_async_remote_copy(
            src_ref=src, dst_ref=dst, send_sem=gather_send, recv_sem=sem,
            device_id=device, device_id_type=MESH,
        )

    def arrived(ref, sem):
        pltpu.make_async_copy(ref, ref, sem).wait()

    sent = []

    def send(*copy):
        remote(*copy).start()
        sent.append(copy)

    home = every.at[y, x * nz + z, mine]
    own = pltpu.make_async_copy(traces, home, own_sem.at[0])
    own.start()
    for far in sorted(range(1, nz), key=lambda far: -ring_far(far, nz)):
        send(traces, home, z_sem, at_z(far))
    wide_part = wide.at[:, pl.ds(pl.multiple_of(y * span, span), span)]
    own_wide = pltpu.make_async_copy(frames, wide_part, own_sem.at[1])
    own_wide.start()
    for far in range(1, ny):
        send(frames, wide_part, wide_sem, at_y(far))

    row = lax.broadcasted_iota(jnp.int32, (BLK, BLK), 0)
    column = lax.broadcasted_iota(jnp.int32, (BLK, BLK), 1)
    ids = lax.broadcasted_iota(jnp.int32, (BLK, neurons), 1)

    def hits(line):
        upright = jnp.sum(jnp.where(row == column, line, 0), axis=1, keepdims=True)
        return jnp.where(upright == ids, 1.0, 0.0)

    for b in range(blocks):
        onehot[b * BLK:(b + 1) * BLK, :] = hits(order[b]).astype(BF16)
    listed = jnp.zeros((1, neurons), F32)
    for b in range(support.shape[0]):
        listed = jnp.maximum(listed, jnp.max(hits(support[b]), axis=0, keepdims=True))
    listed = dot_t(jnp.broadcast_to(listed, (8, neurons)).astype(BF16), onehot[...])
    for b in range(blocks):
        kept[b] = listed[:1, b * BLK:(b + 1) * BLK]
    old = footprints[...]
    hi, lo = split2(old)
    fhi[...] = dot_t(hi, onehot[...]).astype(BF16)
    flo[...] = dot_t(lo, onehot[...]).astype(BF16)

    own.wait()
    own_wide.wait()

    def low(ay, ax):
        return every.at[ay, pl.ds(ax * nz, half), mine]

    def high(ay, ax):
        return every.at[ay, pl.ds(ax * nz + half, half), mine]

    arrived(every.at[y, pl.ds(0, nz - 1), mine], z_sem)
    for far in range(1, nx):
        send(low(y, x), low(y, x), first_sem.at[0, far - 1], at_x(far))
    for far in range(1, ny):
        send(high(y, x), high(y, x), first_sem.at[1, far - 1], at_y(far))

    def finish(kind, part, ref):
        if nc > 1:
            send(ref, ref, core_sem.at[kind, part], other_core)

    def pass_on(kind, part, ref):
        peers, name = (ny, at_y) if kind == 0 else (nx, at_x)
        for far in range(1, peers):
            send(ref, ref, second_sem.at[kind, far - 1, part], name(far))
        finish(kind, part, ref)

    pass_on(0, 0, low(y, x))
    pass_on(1, 0, high(y, x))
    for far in range(1, max(nx, ny)):
        if far < nx:
            ref = low(y, (x + nx - far) % nx)
            arrived(ref, first_sem.at[0, far - 1])
            pass_on(0, far, ref)
        if far < ny:
            ref = high((y + ny - far) % ny, x)
            arrived(ref, first_sem.at[1, far - 1])
            pass_on(1, far, ref)
    for part in range(max(nx, ny)):
        for far in range(1, max(nx, ny)):
            if part < nx and far < ny:
                ref = low((y + ny - far) % ny, (x + nx - part) % nx)
                arrived(ref, second_sem.at[0, far - 1, part])
                finish(0, nx * far + part, ref)
            if part < ny and far < nx:
                ref = high((y + ny - part) % ny, (x + nx - far) % nx)
                arrived(ref, second_sem.at[1, far - 1, part])
                finish(1, ny * far + part, ref)
    if nc > 1:
        for part in range(nx * ny):
            arrived(low(0, 0), core_sem.at[0, part])
            arrived(high(0, 0), core_sem.at[1, part])
    arrived(wide.at[:, pl.ds(0, (ny - 1) * span)], wide_sem)

    def base_copy(i):
        return pltpu.make_async_remote_copy(
            src_ref=bases.at[i], dst_ref=planes.at[i, z // ny],
            send_sem=base_send, recv_sem=base_sem.at[i],
            device_id=place(x, y, 0, c), device_id_type=MESH,
        )

    sends_base = jnp.logical_and(z % ny == y, z != 0)
    keeps_base = jnp.logical_and(y == 0, on_plane)

    def lanes(b):
        return pl.ds(pl.multiple_of(b * BLK, BLK), BLK)

    def hand_over(i):
        @pl.when(sends_base)
        def _():
            base_copy(i).start()

        @pl.when(keeps_base)
        def _():
            pltpu.make_async_copy(bases.at[i], planes.at[i, 0], base_sem.at[i]).start()

    width = min(256, neurons)

    @pl.loop(0, ny * span // width)
    def _(q):
        block = every[q * width // span, :, :, pl.ds(pl.multiple_of(q * width % span, width), width)]
        block = block.reshape(neurons, width)
        ordered[:, pl.ds(pl.multiple_of(q * width, width), width)] = dot(onehot[...], block).astype(BF16)

    @pl.loop(0, neurons // width)
    def _(q):
        some = ordered[pl.ds(pl.multiple_of(q * width, width), width), :]
        gram = dot_t(ordered[...], some)
        row = lax.broadcasted_iota(jnp.int32, gram.shape, 0)
        column = lax.broadcasted_iota(jnp.int32, gram.shape, 1) + q * width
        same = row == column
        diagonal = jnp.sum(jnp.where(same, gram, 0.0), axis=0, keepdims=True)
        hi, lo = split2(jnp.where(same, 0.0, gram) / diagonal)
        start = dot_t(wide[...], some) / diagonal
        for i in range(width // BLK):
            part = slice(i * BLK, (i + 1) * BLK)
            b = q * (width // BLK) + i
            mhi[b] = hi[:, part]
            mlo[b] = lo[:, part]
            base = jnp.where(kept[b] > 0.0, start[:, part], -jnp.inf)
            bases[blocks + b] = base
            bases[b] = base - dot3(fhi[...], flo[...], mhi[b], mlo[b])
            hand_over(b)
            fhi[:, lanes(b)] = jnp.zeros((rows, BLK), BF16)
            flo[:, lanes(b)] = jnp.zeros((rows, BLK), BF16)

    @pl.loop(blocks, 2 * blocks)
    def _(b):
        hand_over(b)

    def base_index(t):
        return jnp.where(t < blocks, t, blocks + t % blocks)

    def sum_copy(t, offset):
        return pltpu.make_async_remote_copy(
            src_ref=sums.at[t], dst_ref=slots.at[t, me],
            send_sem=sum_send.at[t], recv_sem=sum_sem.at[t],
            device_id=peer(offset), device_id_type=MESH,
        )

    def scale_copy(t, far):
        return pltpu.make_async_remote_copy(
            src_ref=scales.at[t], dst_ref=scales.at[t],
            send_sem=scale_send.at[t], recv_sem=scale_sem.at[t],
            device_id=place(x, y, far, c), device_id_type=MESH,
        )

    oupd[...] = jnp.maximum(bases[0], 0.0)
    out[...] = jnp.zeros_like(out)
    ohi[...] = jnp.zeros_like(ohi)
    olo[...] = jnp.zeros_like(olo)

    def replay(t):
        b = t % blocks
        now = oupd[...] * scales[t]
        hi, lo = split2(now)
        ohi[:, lanes(b)] = hi
        olo[:, lanes(b)] = lo

        @pl.when(t >= steps - blocks)
        def _():
            rest = ((now - hi.astype(F32)) - lo.astype(F32)).astype(BF16)
            back = onehot[lanes(b), :]
            out[...] += (dot(hi, back) + dot(lo, back)) + dot(rest, back)

        @pl.when(t < steps - 1)
        def _():
            nxt = (t + 1) % blocks
            value = bases[base_index(t + 1)] - dot3(ohi[...], olo[...], mhi[nxt], mlo[nxt])
            oupd[...] = jnp.maximum(value, 0.0)

    def emit(t):
        new = jnp.maximum(acc[...], 0.0)
        upd[...] = new
        total = jnp.sum(new * new, axis=0, keepdims=True)
        sums[t] = total
        slots[t, me] = total
        for offset in offsets:
            sum_copy(t, offset).start()

    def prepare(t):
        @pl.when(t < 2 * blocks)
        def _():
            pltpu.make_async_copy(planes.at[t], planes.at[t], base_sem.at[t]).wait()
        return planes[base_index(t)].reshape(group * rows, BLK)

    def receive(t):
        waited = slots.at[t, pl.ds(0, devices - 1)]
        pltpu.make_async_copy(waited, waited, sum_sem.at[t]).wait()
        squares = jnp.sum(slots[t], axis=0)
        inverse = 1.0 / jnp.sqrt(squares / pixels + 1e-06)
        scales[t] = inverse
        return inverse

    def ahead(t):
        b = t % blocks
        nxt = (t + 1) % blocks
        chi[:, lanes(b)] = jnp.zeros((group * rows, BLK), BF16)
        clo[:, lanes(b)] = jnp.zeros((group * rows, BLK), BF16)
        base = prepare(t + 1)
        acc[...] = base - dot3(chi[...], clo[...], mhi[nxt], mlo[nxt])

    def share(t):
        for far in range(nz - 1, 0, -1):
            scale_copy(t, far).start()
        replay(t)

    @pl.when(on_plane)
    def _():
        chi[...] = jnp.zeros_like(chi)
        clo[...] = jnp.zeros_like(clo)
        acc[...] = prepare(0)
        emit(0)
        ahead(0)

        @pl.loop(1, steps)
        def _(t):
            prev, b = (t - 1) % blocks, t % blocks
            now = upd[...] * receive(t - 1)
            hi, lo = split2(now)
            inner = pl.ds(pl.multiple_of(prev * BLK, BLK), BLK)
            acc[...] = acc[...] - dot3(hi, lo, mhi[b, inner], mlo[b, inner])
            emit(t)
            chi[:, lanes(prev)] = hi
            clo[:, lanes(prev)] = lo
            share(t - 1)

            @pl.when(t < steps - 1)
            def _():
                ahead(t)

        receive(steps - 1)
        share(steps - 1)

        @pl.loop(0, steps)
        def _(t):
            for offset in offsets:
                sum_copy(t, offset).wait_send()
            for far in range(nz - 1, 0, -1):
                scale_copy(t, far).wait_send()

    @pl.when(z != 0)
    def _():
        @pl.loop(0, steps)
        def _(t):
            pltpu.make_async_copy(scales.at[t], scales.at[t], scale_sem.at[t]).wait()
            replay(t)

    @pl.when(sends_base)
    def _():
        for i in range(2 * blocks):
            base_copy(i).wait_send()

    for copy in sent:
        remote(*copy).wait_send()


def local(dims, frames_y, traces, footprints, order, support):
    nx, ny, nz, nc = dims
    rows, span = frames_y.shape
    slab = traces.shape[0]
    neurons = footprints.shape[1]
    blocks = neurons // BLK
    steps = SWEEPS * blocks
    group = nz // ny
    devices = nx * ny * nc
    pixels = rows * lax.axis_size("pix")
    listed = -(-support.shape[1] // BLK)
    support = jnp.pad(support[0], (0, listed * BLK - support.shape[1]), constant_values=-1)
    dma = pltpu.SemaphoreType.DMA
    most = max(nx, ny)
    return pl.pallas_call(
        functools.partial(cnmf_kernel, dims, pixels),
        out_shape=jax.ShapeDtypeStruct((rows, neurons), F32),
        in_specs=[pl.BlockSpec(memory_space=pltpu.VMEM)] * 5,
        out_specs=pl.BlockSpec(memory_space=pltpu.VMEM),
        scratch_shapes=[
            pltpu.VMEM((neurons, neurons), BF16),
            pltpu.VMEM((blocks, 1, BLK), F32),
            pltpu.VMEM((ny, nx * nz, nc * slab, span), BF16),
            pltpu.VMEM((rows, ny * span), BF16),
            pltpu.VMEM((neurons, ny * span), BF16),
            pltpu.VMEM((rows, neurons), BF16),
            pltpu.VMEM((rows, neurons), BF16),
            pltpu.VMEM((2 * blocks, rows, BLK), F32),
            pltpu.VMEM((blocks, neurons, BLK), BF16),
            pltpu.VMEM((blocks, neurons, BLK), BF16),
            dma((2,)),
            dma,
            dma,
            dma((2, most - 1)),
            dma((2, most - 1, most)),
            dma((2, nx * ny)),
            dma,
            pltpu.VMEM((2 * blocks, group, rows, BLK), F32),
            pltpu.VMEM((steps, devices, 1, BLK), F32),
            pltpu.VMEM((steps, 1, BLK), F32),
            pltpu.VMEM((steps, 1, BLK), F32),
            pltpu.VMEM((group * rows, BLK), F32),
            pltpu.VMEM((group * rows, BLK), F32),
            pltpu.VMEM((group * rows, neurons), BF16),
            pltpu.VMEM((group * rows, neurons), BF16),
            pltpu.VMEM((rows, BLK), F32),
            pltpu.VMEM((rows, neurons), BF16),
            pltpu.VMEM((rows, neurons), BF16),
            dma((2 * blocks,)),
            dma,
            dma((steps,)),
            dma((steps,)),
            dma((steps,)),
            dma((steps,)),
        ],
        compiler_params=pltpu.CompilerParams(collective_id=1, has_side_effects=True),
        name="cnmf",
    )(frames_y, traces, footprints, order.reshape(blocks, 1, BLK), support.reshape(listed, 1, BLK))


def solution(mesh, dims=DIMS):
    placed = (P("pix", "frm"), P("pix", "frm"), P("pix", None), P(), P("pix", None))
    return jax.shard_map(
        functools.partial(local, dims), mesh=mesh, in_specs=placed,
        out_specs=P("pix", None), check_vma=False,
    )
```

```python
import functools

import jax
import jax.numpy as jnp
from jax import lax
from jax.experimental import pallas as pl
from jax.experimental.pallas import tpu as pltpu
from jax.sharding import PartitionSpec as P

BLK = 128
SWEEPS = 3
DIMS = (4, 4, 16, 2)
PLANES = 2
MESH = pl.DeviceIdType.MESH
F32, BF16 = jnp.float32, jnp.bfloat16


def ring_far(d, n):
    return min(d, n - d)


def plane_offsets(nx, ny, nc):
    every = [
        (dx, dy, dc)
        for dx in range(nx)
        for dy in range(ny)
        for dc in range(nc)
        if (dx, dy, dc) != (0, 0, 0)
    ]
    return sorted(every, key=lambda o: -(ring_far(o[0], nx) + ring_far(o[1], ny) + 0.1 * o[2]))


def split2(v):
    hi = v.astype(BF16)
    return hi, (v - hi.astype(F32)).astype(BF16)


def dot(a, b):
    return lax.dot_general(a, b, (((1,), (0,)), ((), ())), preferred_element_type=F32)


def dot3(ahi, alo, bhi, blo):
    return dot(ahi, bhi) + (dot(ahi, blo) + dot(alo, bhi))


def dot_t(a, b):
    return lax.dot_general(a, b, (((1,), (1,)), ((), ())), preferred_element_type=F32)


def cnmf_kernel(
    dims, pixels,
    frames, traces, footprints, order, support, out,
    onehot, kept, every, wide, ordered, fhi, flo, bases, mhi, mlo,
    own_sem, wide_sem, z_sem, first_sem, second_sem, core_sem, gather_send,
    planes, slots, sums, scales, acc, upd, chi, clo, oupd, ohi, olo,
    base_sem, base_send, sum_sem, sum_send, scale_sem, scale_send,
):
    nx, ny, nz, nc = dims
    group = nz // ny
    rows, neurons = out.shape
    blocks = neurons // BLK
    steps = SWEEPS * blocks
    devices = nx * ny * nc
    half = nz // 2
    slab, span = traces.shape
    pix, y = lax.axis_index("pix"), lax.axis_index("frm")
    x, z, c = pix // (nz * nc), (pix // nc) % nz, pix % nc
    me = (x * ny + y) * nc + c
    hop = nz // PLANES
    shift = (hop - 1) // 2
    on_plane = z % hop == 0
    follow = sorted((d for d in range(-shift, hop - shift) if d), key=lambda d: -abs(d))
    offsets = plane_offsets(nx, ny, nc)

    def place(ax, ay, az, ac):
        return ((ax * nz + az) * nc + ac, ay)

    def peer(offset):
        return place((x + offset[0]) % nx, (y + offset[1]) % ny, z, (c + offset[2]) % nc)

    barrier = pltpu.get_barrier_semaphore()

    def at_z(far):
        return place(x, y, (z + far) % nz, c)

    def at_x(far):
        return place((x + far) % nx, y, z, c)

    def at_y(far):
        return place(x, (y + far) % ny, z, c)

    other_core = place(x, y, z, (c + 1) % nc)
    near = (
        [at_z(far) for far in range(1, nz)]
        + [at_x(far) for far in range(1, nx)]
        + [at_y(far) for far in range(1, ny)]
        + [other_core] * (nc - 1)
    )
    apart = [o for o in offsets if (o[0] != 0) + (o[1] != 0) + (o[2] != 0) > 1]

    def greet(devices):
        for device in devices:
            pl.semaphore_signal(barrier, inc=1, device_id=device, device_id_type=MESH)

    greet(near)

    @pl.when(on_plane)
    def _():
        greet([peer(offset) for offset in apart])
        pl.semaphore_wait(barrier, len(near) + len(apart))

    @pl.when(jnp.logical_not(on_plane))
    def _():
        pl.semaphore_wait(barrier, len(near))

    mine = pl.ds(pl.multiple_of(c * slab, slab), slab)

    def remote(src, dst, sem, device):
        return pltpu.make_async_remote_copy(
            src_ref=src, dst_ref=dst, send_sem=gather_send, recv_sem=sem,
            device_id=device, device_id_type=MESH,
        )

    def arrived(ref, sem):
        pltpu.make_async_copy(ref, ref, sem).wait()

    sent = []

    def send(*copy):
        remote(*copy).start()
        sent.append(copy)

    home = every.at[y, x * nz + z, mine]
    own = pltpu.make_async_copy(traces, home, own_sem.at[0])
    own.start()
    for far in sorted(range(1, nz), key=lambda far: -ring_far(far, nz)):
        send(traces, home, z_sem, at_z(far))
    wide_part = wide.at[:, pl.ds(pl.multiple_of(y * span, span), span)]
    own_wide = pltpu.make_async_copy(frames, wide_part, own_sem.at[1])
    own_wide.start()
    for far in range(1, ny):
        send(frames, wide_part, wide_sem, at_y(far))

    row = lax.broadcasted_iota(jnp.int32, (BLK, BLK), 0)
    column = lax.broadcasted_iota(jnp.int32, (BLK, BLK), 1)
    ids = lax.broadcasted_iota(jnp.int32, (BLK, neurons), 1)

    def hits(line):
        upright = jnp.sum(jnp.where(row == column, line, 0), axis=1, keepdims=True)
        return jnp.where(upright == ids, 1.0, 0.0)

    for b in range(blocks):
        onehot[b * BLK:(b + 1) * BLK, :] = hits(order[b]).astype(BF16)
    listed = jnp.zeros((1, neurons), F32)
    for b in range(support.shape[0]):
        listed = jnp.maximum(listed, jnp.max(hits(support[b]), axis=0, keepdims=True))
    listed = dot_t(jnp.broadcast_to(listed, (8, neurons)).astype(BF16), onehot[...])
    for b in range(blocks):
        kept[b] = listed[:1, b * BLK:(b + 1) * BLK]
    old = footprints[...]
    hi, lo = split2(old)
    fhi[...] = dot_t(hi, onehot[...]).astype(BF16)
    flo[...] = dot_t(lo, onehot[...]).astype(BF16)

    own.wait()
    own_wide.wait()

    def low(ay, ax):
        return every.at[ay, pl.ds(ax * nz, half), mine]

    def high(ay, ax):
        return every.at[ay, pl.ds(ax * nz + half, half), mine]

    arrived(every.at[y, pl.ds(0, nz - 1), mine], z_sem)
    for far in range(1, nx):
        send(low(y, x), low(y, x), first_sem.at[0, far - 1], at_x(far))
    for far in range(1, ny):
        send(high(y, x), high(y, x), first_sem.at[1, far - 1], at_y(far))

    def finish(kind, part, ref):
        if nc > 1:
            send(ref, ref, core_sem.at[kind, part], other_core)

    def pass_on(kind, part, ref):
        peers, name = (ny, at_y) if kind == 0 else (nx, at_x)
        for far in range(1, peers):
            send(ref, ref, second_sem.at[kind, far - 1, part], name(far))
        finish(kind, part, ref)

    pass_on(0, 0, low(y, x))
    pass_on(1, 0, high(y, x))
    for far in range(1, max(nx, ny)):
        if far < nx:
            ref = low(y, (x + nx - far) % nx)
            arrived(ref, first_sem.at[0, far - 1])
            pass_on(0, far, ref)
        if far < ny:
            ref = high((y + ny - far) % ny, x)
            arrived(ref, first_sem.at[1, far - 1])
            pass_on(1, far, ref)
    for part in range(max(nx, ny)):
        for far in range(1, max(nx, ny)):
            if part < nx and far < ny:
                ref = low((y + ny - far) % ny, (x + nx - part) % nx)
                arrived(ref, second_sem.at[0, far - 1, part])
                finish(0, nx * far + part, ref)
            if part < ny and far < nx:
                ref = high((y + ny - part) % ny, (x + nx - far) % nx)
                arrived(ref, second_sem.at[1, far - 1, part])
                finish(1, ny * far + part, ref)
    if nc > 1:
        for part in range(nx * ny):
            arrived(low(0, 0), core_sem.at[0, part])
            arrived(high(0, 0), core_sem.at[1, part])
    arrived(wide.at[:, pl.ds(0, (ny - 1) * span)], wide_sem)

    def base_copy(i, plane):
        return pltpu.make_async_remote_copy(
            src_ref=bases.at[i], dst_ref=planes.at[i, z // ny],
            send_sem=base_send, recv_sem=base_sem.at[i],
            device_id=place(x, y, plane * hop, c), device_id_type=MESH,
        )

    gives = z % ny == y

    def lanes(b):
        return pl.ds(pl.multiple_of(b * BLK, BLK), BLK)

    def hand_over(i):
        for plane in range(PLANES):
            @pl.when(jnp.logical_and(gives, z != plane * hop))
            def _():
                base_copy(i, plane).start()

            @pl.when(jnp.logical_and(gives, z == plane * hop))
            def _():
                pltpu.make_async_copy(bases.at[i], planes.at[i, z // ny], base_sem.at[i]).start()

    def handed_over():
        for plane in range(PLANES):
            @pl.when(jnp.logical_and(gives, z != plane * hop))
            def _():
                for i in range(2 * blocks):
                    base_copy(i, plane).wait_send()

    width = min(256, neurons)

    @pl.loop(0, ny * span // width)
    def _(q):
        block = every[q * width // span, :, :, pl.ds(pl.multiple_of(q * width % span, width), width)]
        block = block.reshape(neurons, width)
        ordered[:, pl.ds(pl.multiple_of(q * width, width), width)] = dot(onehot[...], block).astype(BF16)

    @pl.loop(0, neurons // width)
    def _(q):
        some = ordered[pl.ds(pl.multiple_of(q * width, width), width), :]
        gram = dot_t(ordered[...], some)
        row = lax.broadcasted_iota(jnp.int32, gram.shape, 0)
        column = lax.broadcasted_iota(jnp.int32, gram.shape, 1) + q * width
        same = row == column
        diagonal = jnp.sum(jnp.where(same, gram, 0.0), axis=0, keepdims=True)
        hi, lo = split2(jnp.where(same, 0.0, gram) / diagonal)
        start = dot_t(wide[...], some) / diagonal
        for i in range(width // BLK):
            part = slice(i * BLK, (i + 1) * BLK)
            b = q * (width // BLK) + i
            mhi[b] = hi[:, part]
            mlo[b] = lo[:, part]
            base = jnp.where(kept[b] > 0.0, start[:, part], -jnp.inf)
            bases[blocks + b] = base
            bases[b] = base - dot3(fhi[...], flo[...], mhi[b], mlo[b])
            hand_over(b)
            fhi[:, lanes(b)] = jnp.zeros((rows, BLK), BF16)
            flo[:, lanes(b)] = jnp.zeros((rows, BLK), BF16)

    @pl.loop(blocks, 2 * blocks)
    def _(b):
        hand_over(b)

    for copy in sent:
        remote(*copy).wait_send()

    def base_index(t):
        return jnp.where(t < blocks, t, blocks + t % blocks)

    def sum_copy(t, offset):
        return pltpu.make_async_remote_copy(
            src_ref=sums.at[t], dst_ref=slots.at[t, me],
            send_sem=sum_send.at[t], recv_sem=sum_sem.at[t],
            device_id=peer(offset), device_id_type=MESH,
        )

    def scale_copy(t, far):
        return pltpu.make_async_remote_copy(
            src_ref=scales.at[t], dst_ref=scales.at[t],
            send_sem=scale_send.at[t], recv_sem=scale_sem.at[t],
            device_id=place(x, y, (z + far + nz) % nz, c), device_id_type=MESH,
        )

    oupd[...] = jnp.maximum(bases[0], 0.0)
    out[...] = jnp.zeros_like(out)
    ohi[...] = jnp.zeros_like(ohi)
    olo[...] = jnp.zeros_like(olo)

    def replay(t):
        b = t % blocks
        now = oupd[...] * scales[t]
        hi, lo = split2(now)
        ohi[:, lanes(b)] = hi
        olo[:, lanes(b)] = lo

        @pl.when(t >= steps - blocks)
        def _():
            rest = ((now - hi.astype(F32)) - lo.astype(F32)).astype(BF16)
            back = onehot[lanes(b), :]
            out[...] += (dot(hi, back) + dot(lo, back)) + dot(rest, back)

        @pl.when(t < steps - 1)
        def _():
            nxt = (t + 1) % blocks
            value = bases[base_index(t + 1)] - dot3(ohi[...], olo[...], mhi[nxt], mlo[nxt])
            oupd[...] = jnp.maximum(value, 0.0)

    def emit(t):
        new = jnp.maximum(acc[...], 0.0)
        upd[...] = new
        total = jnp.sum(new * new, axis=0, keepdims=True)
        sums[t] = total
        slots[t, me] = total
        for offset in offsets:
            sum_copy(t, offset).start()

    def prepare(t):
        @pl.when(t < 2 * blocks)
        def _():
            pltpu.make_async_copy(planes.at[t], planes.at[t], base_sem.at[t]).wait()
        return planes[base_index(t)].reshape(group * rows, BLK)

    def receive(t):
        waited = slots.at[t, pl.ds(0, devices - 1)]
        pltpu.make_async_copy(waited, waited, sum_sem.at[t]).wait()
        squares = jnp.sum(slots[t], axis=0)
        inverse = 1.0 / jnp.sqrt(squares / pixels + 1e-06)
        scales[t] = inverse
        return inverse

    def ahead(t):
        b = t % blocks
        nxt = (t + 1) % blocks
        chi[:, lanes(b)] = jnp.zeros((group * rows, BLK), BF16)
        clo[:, lanes(b)] = jnp.zeros((group * rows, BLK), BF16)
        base = prepare(t + 1)
        acc[...] = base - dot3(chi[...], clo[...], mhi[nxt], mlo[nxt])

    def share(t):
        for far in follow:
            scale_copy(t, far).start()
        replay(t)

    @pl.when(on_plane)
    def _():
        chi[...] = jnp.zeros_like(chi)
        clo[...] = jnp.zeros_like(clo)
        acc[...] = prepare(0)
        emit(0)
        ahead(0)

        @pl.loop(1, steps)
        def _(t):
            prev, b = (t - 1) % blocks, t % blocks
            now = upd[...] * receive(t - 1)
            hi, lo = split2(now)
            inner = pl.ds(pl.multiple_of(prev * BLK, BLK), BLK)
            acc[...] = acc[...] - dot3(hi, lo, mhi[b, inner], mlo[b, inner])
            emit(t)
            chi[:, lanes(prev)] = hi
            clo[:, lanes(prev)] = lo
            share(t - 1)

            @pl.when(t < steps - 1)
            def _():
                ahead(t)

        handed_over()
        receive(steps - 1)
        share(steps - 1)

        @pl.loop(0, steps)
        def _(t):
            gone = slots.at[t, pl.ds(0, devices - 1)]
            pltpu.make_async_copy(gone, gone, sum_send.at[t]).wait()
            if follow:
                gone = slots.at[t, pl.ds(0, len(follow))]
                pltpu.make_async_copy(gone, gone, scale_send.at[t]).wait()

    @pl.when(jnp.logical_not(on_plane))
    def _():
        @pl.loop(0, steps)
        def _(t):
            @pl.when(t == steps - 1)
            def _():
                handed_over()
            pltpu.make_async_copy(scales.at[t], scales.at[t], scale_sem.at[t]).wait()
            replay(t)


def local(dims, frames_y, traces, footprints, order, support):
    nx, ny, nz, nc = dims
    rows, span = frames_y.shape
    slab = traces.shape[0]
    neurons = footprints.shape[1]
    blocks = neurons // BLK
    steps = SWEEPS * blocks
    group = nz // ny
    devices = nx * ny * nc
    pixels = rows * lax.axis_size("pix")
    listed = -(-support.shape[1] // BLK)
    support = jnp.pad(support[0], (0, listed * BLK - support.shape[1]), constant_values=-1)
    dma = pltpu.SemaphoreType.DMA
    most = max(nx, ny)
    return pl.pallas_call(
        functools.partial(cnmf_kernel, dims, pixels),
        out_shape=jax.ShapeDtypeStruct((rows, neurons), F32),
        in_specs=[pl.BlockSpec(memory_space=pltpu.VMEM)] * 5,
        out_specs=pl.BlockSpec(memory_space=pltpu.VMEM),
        scratch_shapes=[
            pltpu.VMEM((neurons, neurons), BF16),
            pltpu.VMEM((blocks, 1, BLK), F32),
            pltpu.VMEM((ny, nx * nz, nc * slab, span), BF16),
            pltpu.VMEM((rows, ny * span), BF16),
            pltpu.VMEM((neurons, ny * span), BF16),
            pltpu.VMEM((rows, neurons), BF16),
            pltpu.VMEM((rows, neurons), BF16),
            pltpu.VMEM((2 * blocks, rows, BLK), F32),
            pltpu.VMEM((blocks, neurons, BLK), BF16),
            pltpu.VMEM((blocks, neurons, BLK), BF16),
            dma((2,)),
            dma,
            dma,
            dma((2, most - 1)),
            dma((2, most - 1, most)),
            dma((2, nx * ny)),
            dma,
            pltpu.VMEM((2 * blocks, group, rows, BLK), F32),
            pltpu.VMEM((steps, devices, 1, BLK), F32),
            pltpu.VMEM((steps, 1, BLK), F32),
            pltpu.VMEM((steps, 1, BLK), F32),
            pltpu.VMEM((group * rows, BLK), F32),
            pltpu.VMEM((group * rows, BLK), F32),
            pltpu.VMEM((group * rows, neurons), BF16),
            pltpu.VMEM((group * rows, neurons), BF16),
            pltpu.VMEM((rows, BLK), F32),
            pltpu.VMEM((rows, neurons), BF16),
            pltpu.VMEM((rows, neurons), BF16),
            dma((2 * blocks,)),
            dma,
            dma((steps,)),
            dma((steps,)),
            dma((steps,)),
            dma((steps,)),
        ],
        compiler_params=pltpu.CompilerParams(collective_id=1, has_side_effects=True),
        name="cnmf",
    )(frames_y, traces, footprints, order.reshape(blocks, 1, BLK), support.reshape(listed, 1, BLK))


def solution(mesh, dims=DIMS):
    placed = (P("pix", "frm"), P("pix", "frm"), P("pix", None), P(), P("pix", None))
    return jax.shard_map(
        functools.partial(local, dims), mesh=mesh, in_specs=placed,
        out_specs=P("pix", None), check_vma=False,
    )
```

```python
import functools

import jax
import jax.numpy as jnp
from jax import lax
from jax.experimental import pallas as pl
from jax.experimental.pallas import tpu as pltpu
from jax.sharding import PartitionSpec as P

BLK = 128
SWEEPS = 3
DIMS = (4, 4, 16, 2)
PLANES = 1
MESH = pl.DeviceIdType.MESH
F32, BF16 = jnp.float32, jnp.bfloat16


def ring_far(d, n):
    return min(d, n - d)


def plane_offsets(nx, ny, nc):
    every = [
        (dx, dy, dc)
        for dx in range(nx)
        for dy in range(ny)
        for dc in range(nc)
        if (dx, dy, dc) != (0, 0, 0)
    ]
    return sorted(every, key=lambda o: -(ring_far(o[0], nx) + ring_far(o[1], ny) + 0.1 * o[2]))


def split2(v):
    hi = v.astype(BF16)
    return hi, (v - hi.astype(F32)).astype(BF16)


def dot(a, b):
    return lax.dot_general(a, b, (((1,), (0,)), ((), ())), preferred_element_type=F32)


def dot3(ahi, alo, bhi, blo):
    return dot(ahi, bhi) + (dot(ahi, blo) + dot(alo, bhi))


def dot_t(a, b):
    return lax.dot_general(a, b, (((1,), (1,)), ((), ())), preferred_element_type=F32)


def cnmf_kernel(
    dims, pixels,
    frames, traces, footprints, order, support, out,
    onehot, kept, nhi, nlo, every, wide, ordered, fhi, flo, bases, mhi, mlo,
    own_sem, wide_sem, z_sem, first_sem, second_sem, core_sem, gather_send,
    planes, slots, sums, scales, acc, upd, chi, clo, oupd, ohi, olo,
    base_sem, base_send, sum_sem, sum_send, scale_sem, scale_send,
):
    nx, ny, nz, nc = dims
    group = nz // ny
    rows, neurons = out.shape
    blocks = neurons // BLK
    steps = SWEEPS * blocks
    devices = nx * ny * nc
    half = nz // 2
    slab, span = traces.shape
    pix, y = lax.axis_index("pix"), lax.axis_index("frm")
    x, z, c = pix // (nz * nc), (pix // nc) % nz, pix % nc
    me = (x * ny + y) * nc + c
    hop = nz // PLANES
    shift = (hop - 1) // 2
    on_plane = z % hop == 0
    follow = sorted((d for d in range(-shift, hop - shift) if d), key=lambda d: -abs(d))
    offsets = plane_offsets(nx, ny, nc)

    def place(ax, ay, az, ac):
        return ((ax * nz + az) * nc + ac, ay)

    def peer(offset):
        return place((x + offset[0]) % nx, (y + offset[1]) % ny, z, (c + offset[2]) % nc)

    barrier = pltpu.get_barrier_semaphore()

    def at_z(far):
        return place(x, y, (z + far) % nz, c)

    def at_x(far):
        return place((x + far) % nx, y, z, c)

    def at_y(far):
        return place(x, (y + far) % ny, z, c)

    other_core = place(x, y, z, (c + 1) % nc)
    near = (
        [at_z(far) for far in range(1, nz)]
        + [at_x(far) for far in range(1, nx)]
        + [at_y(far) for far in range(1, ny)]
        + [other_core] * (nc - 1)
    )
    apart = [o for o in offsets if (o[0] != 0) + (o[1] != 0) + (o[2] != 0) > 1]

    def greet(devices):
        for device in devices:
            pl.semaphore_signal(barrier, inc=1, device_id=device, device_id_type=MESH)

    greet(near)

    @pl.when(on_plane)
    def _():
        greet([peer(offset) for offset in apart])
        pl.semaphore_wait(barrier, len(near) + len(apart))

    @pl.when(jnp.logical_not(on_plane))
    def _():
        pl.semaphore_wait(barrier, len(near))

    mine = pl.ds(pl.multiple_of(c * slab, slab), slab)

    def remote(src, dst, sem, device):
        return pltpu.make_async_remote_copy(
            src_ref=src, dst_ref=dst, send_sem=gather_send, recv_sem=sem,
            device_id=device, device_id_type=MESH,
        )

    def arrived(ref, sem):
        pltpu.make_async_copy(ref, ref, sem).wait()

    sent = []

    def send(*copy):
        remote(*copy).start()
        sent.append(copy)

    home = every.at[y, x * nz + z, mine]
    own = pltpu.make_async_copy(traces, home, own_sem.at[0])
    own.start()
    for far in sorted(range(1, nz), key=lambda far: -ring_far(far, nz)):
        send(traces, home, z_sem, at_z(far))
    wide_part = wide.at[:, pl.ds(pl.multiple_of(y * span, span), span)]
    own_wide = pltpu.make_async_copy(frames, wide_part, own_sem.at[1])
    own_wide.start()
    for far in range(1, ny):
        send(frames, wide_part, wide_sem, at_y(far))

    row = lax.broadcasted_iota(jnp.int32, (BLK, BLK), 0)
    column = lax.broadcasted_iota(jnp.int32, (BLK, BLK), 1)
    ids = lax.broadcasted_iota(jnp.int32, (BLK, neurons), 1)

    def hits(line):
        upright = jnp.sum(jnp.where(row == column, line, 0), axis=1, keepdims=True)
        return jnp.where(upright == ids, 1.0, 0.0)

    for b in range(blocks):
        onehot[b * BLK:(b + 1) * BLK, :] = hits(order[b]).astype(BF16)
    listed = jnp.zeros((1, neurons), F32)
    for b in range(support.shape[0]):
        listed = jnp.maximum(listed, jnp.max(hits(support[b]), axis=0, keepdims=True))
    listed = dot_t(jnp.broadcast_to(listed, (8, neurons)).astype(BF16), onehot[...])
    for b in range(blocks):
        kept[b] = listed[:1, b * BLK:(b + 1) * BLK]
    old = footprints[...]
    hi, lo = split2(old)
    nhi[...] = hi
    nlo[...] = lo
    fhi[...] = dot_t(hi, onehot[...]).astype(BF16)
    flo[...] = dot_t(lo, onehot[...]).astype(BF16)

    own.wait()
    own_wide.wait()

    def low(ay, ax):
        return every.at[ay, pl.ds(ax * nz, half), mine]

    def high(ay, ax):
        return every.at[ay, pl.ds(ax * nz + half, half), mine]

    arrived(every.at[y, pl.ds(0, nz - 1), mine], z_sem)
    for far in range(1, nx):
        send(low(y, x), low(y, x), first_sem.at[0, far - 1], at_x(far))
    for far in range(1, ny):
        send(high(y, x), high(y, x), first_sem.at[1, far - 1], at_y(far))

    def finish(kind, part, ref):
        if nc > 1:
            send(ref, ref, core_sem.at[kind, part], other_core)

    def pass_on(kind, part, ref):
        peers, name = (ny, at_y) if kind == 0 else (nx, at_x)
        for far in range(1, peers):
            send(ref, ref, second_sem.at[kind, far - 1, part], name(far))
        finish(kind, part, ref)

    pass_on(0, 0, low(y, x))
    pass_on(1, 0, high(y, x))
    for far in range(1, max(nx, ny)):
        if far < nx:
            ref = low(y, (x + nx - far) % nx)
            arrived(ref, first_sem.at[0, far - 1])
            pass_on(0, far, ref)
        if far < ny:
            ref = high((y + ny - far) % ny, x)
            arrived(ref, first_sem.at[1, far - 1])
            pass_on(1, far, ref)
    for part in range(max(nx, ny)):
        for far in range(1, max(nx, ny)):
            if part < nx and far < ny:
                ref = low((y + ny - far) % ny, (x + nx - part) % nx)
                arrived(ref, second_sem.at[0, far - 1, part])
                finish(0, nx * far + part, ref)
            if part < ny and far < nx:
                ref = high((y + ny - part) % ny, (x + nx - far) % nx)
                arrived(ref, second_sem.at[1, far - 1, part])
                finish(1, ny * far + part, ref)
    if nc > 1:
        for part in range(nx * ny):
            arrived(low(0, 0), core_sem.at[0, part])
            arrived(high(0, 0), core_sem.at[1, part])
    arrived(wide.at[:, pl.ds(0, (ny - 1) * span)], wide_sem)

    def base_copy(i, plane):
        return pltpu.make_async_remote_copy(
            src_ref=bases.at[i], dst_ref=planes.at[i, z // ny],
            send_sem=base_send, recv_sem=base_sem.at[i],
            device_id=place(x, y, plane * hop, c), device_id_type=MESH,
        )

    gives = z % ny == y

    def lanes(b):
        return pl.ds(pl.multiple_of(b * BLK, BLK), BLK)

    def hand_over(i):
        for plane in range(PLANES):
            @pl.when(jnp.logical_and(gives, z != plane * hop))
            def _():
                base_copy(i, plane).start()

            @pl.when(jnp.logical_and(gives, z == plane * hop))
            def _():
                pltpu.make_async_copy(bases.at[i], planes.at[i, z // ny], base_sem.at[i]).start()

    def handed_over():
        for plane in range(PLANES):
            @pl.when(jnp.logical_and(gives, z != plane * hop))
            def _():
                for i in range(2 * blocks):
                    base_copy(i, plane).wait_send()

    width = min(256, neurons)
    per = width // BLK

    @pl.when(jnp.logical_not(on_plane))
    def _():
        gram = jnp.zeros((neurons, width), F32)
        for ay in range(ny):
            block = every[ay].reshape(neurons, span)
            some = dot(onehot[:width, :], block).astype(BF16)
            ordered[:width, ay * span:(ay + 1) * span] = some
            gram = gram + dot_t(block, some)
        some = ordered[:width, :]
        place_of = lax.broadcasted_iota(jnp.int32, (neurons, BLK), 0)
        cross = dot_t(wide[...], some)
        for b in range(per):
            part = slice(b * BLK, (b + 1) * BLK)
            same = place_of == order[b]
            diagonal = jnp.sum(jnp.where(same, gram[:, part], 0.0), axis=0, keepdims=True)
            hi, lo = split2(jnp.where(same, 0.0, gram[:, part]) / diagonal)
            start = jnp.where(kept[b] > 0.0, cross[:, part] / diagonal, -jnp.inf)
            if b == 0:
                ahi, alo = nhi[...], nlo[...]
            else:
                done = jnp.sum(onehot[:b * BLK, :].astype(F32), axis=0, keepdims=True)
                left = (1.0 - done).astype(BF16)
                ahi, alo = nhi[...] * left, nlo[...] * left
            bases[b] = start - dot3(ahi, alo, hi, lo)
            hand_over(b)

    @pl.loop(0, ny * span // width)
    def _(q):
        block = every[q * width // span, :, :, pl.ds(pl.multiple_of(q * width % span, width), width)]
        block = block.reshape(neurons, width)
        ordered[:, pl.ds(pl.multiple_of(q * width, width), width)] = dot(onehot[...], block).astype(BF16)

    def columns(q):
        some = ordered[pl.ds(pl.multiple_of(q * width, width), width), :]
        gram = dot_t(ordered[...], some)
        row = lax.broadcasted_iota(jnp.int32, gram.shape, 0)
        column = lax.broadcasted_iota(jnp.int32, gram.shape, 1) + q * width
        same = row == column
        diagonal = jnp.sum(jnp.where(same, gram, 0.0), axis=0, keepdims=True)
        hi, lo = split2(jnp.where(same, 0.0, gram) / diagonal)
        start = dot_t(wide[...], some) / diagonal
        for i in range(per):
            part = slice(i * BLK, (i + 1) * BLK)
            b = q * per + i
            mhi[b] = hi[:, part]
            mlo[b] = lo[:, part]
            bases[blocks + b] = jnp.where(kept[b] > 0.0, start[:, part], -jnp.inf)

            @pl.when(jnp.logical_or(on_plane, q > 0))
            def _():
                bases[b] = bases[blocks + b] - dot3(fhi[...], flo[...], mhi[b], mlo[b])
                hand_over(b)

            @pl.when(on_plane)
            def _():
                hand_over(blocks + b)

            fhi[:, lanes(b)] = jnp.zeros((rows, BLK), BF16)
            flo[:, lanes(b)] = jnp.zeros((rows, BLK), BF16)

    @pl.loop(0, jnp.where(on_plane, 1, blocks // per))
    def _(q):
        columns(q)

    @pl.when(jnp.logical_not(on_plane))
    def _():
        @pl.loop(blocks, 2 * blocks)
        def _(b):
            hand_over(b)

    for copy in sent:
        remote(*copy).wait_send()

    def base_index(t):
        return jnp.where(t < blocks, t, blocks + t % blocks)

    def sum_copy(t, offset):
        return pltpu.make_async_remote_copy(
            src_ref=sums.at[t], dst_ref=slots.at[t, me],
            send_sem=sum_send.at[t], recv_sem=sum_sem.at[t],
            device_id=peer(offset), device_id_type=MESH,
        )

    def scale_copy(t, far):
        return pltpu.make_async_remote_copy(
            src_ref=scales.at[t], dst_ref=scales.at[t],
            send_sem=scale_send.at[t], recv_sem=scale_sem.at[t],
            device_id=place(x, y, (z + far + nz) % nz, c), device_id_type=MESH,
        )

    oupd[...] = jnp.maximum(bases[0], 0.0)
    out[...] = jnp.zeros_like(out)
    ohi[...] = jnp.zeros_like(ohi)
    olo[...] = jnp.zeros_like(olo)

    def replay(t):
        b = t % blocks
        now = oupd[...] * scales[t]
        hi, lo = split2(now)
        ohi[:, lanes(b)] = hi
        olo[:, lanes(b)] = lo

        @pl.when(t >= steps - blocks)
        def _():
            rest = ((now - hi.astype(F32)) - lo.astype(F32)).astype(BF16)
            back = onehot[lanes(b), :]
            out[...] += (dot(hi, back) + dot(lo, back)) + dot(rest, back)

        @pl.when(t < steps - 1)
        def _():
            nxt = (t + 1) % blocks
            value = bases[base_index(t + 1)] - dot3(ohi[...], olo[...], mhi[nxt], mlo[nxt])
            oupd[...] = jnp.maximum(value, 0.0)

    def emit(t):
        new = jnp.maximum(acc[...], 0.0)
        upd[...] = new
        total = jnp.sum(new * new, axis=0, keepdims=True)
        sums[t] = total
        slots[t, me] = total
        for offset in offsets:
            sum_copy(t, offset).start()

    def prepare(t):
        @pl.when(t < 2 * blocks)
        def _():
            pltpu.make_async_copy(planes.at[t], planes.at[t], base_sem.at[t]).wait()
        return planes[base_index(t)].reshape(group * rows, BLK)

    def receive(t):
        waited = slots.at[t, pl.ds(0, devices - 1)]
        pltpu.make_async_copy(waited, waited, sum_sem.at[t]).wait()
        squares = jnp.sum(slots[t], axis=0)
        inverse = 1.0 / jnp.sqrt(squares / pixels + 1e-06)
        scales[t] = inverse
        return inverse

    def ahead(t):
        b = t % blocks
        nxt = (t + 1) % blocks
        chi[:, lanes(b)] = jnp.zeros((group * rows, BLK), BF16)
        clo[:, lanes(b)] = jnp.zeros((group * rows, BLK), BF16)
        base = prepare(t + 1)
        acc[...] = base - dot3(chi[...], clo[...], mhi[nxt], mlo[nxt])

    def share(t):
        for far in follow:
            scale_copy(t, far).start()
        replay(t)

    @pl.when(on_plane)
    def _():
        chi[...] = jnp.zeros_like(chi)
        clo[...] = jnp.zeros_like(clo)
        acc[...] = prepare(0)
        emit(0)
        ahead(0)

        @pl.loop(1, steps)
        def _(t):
            prev, b = (t - 1) % blocks, t % blocks
            now = upd[...] * receive(t - 1)
            hi, lo = split2(now)
            inner = pl.ds(pl.multiple_of(prev * BLK, BLK), BLK)
            acc[...] = acc[...] - dot3(hi, lo, mhi[b, inner], mlo[b, inner])
            emit(t)
            chi[:, lanes(prev)] = hi
            clo[:, lanes(prev)] = lo
            share(t - 1)

            @pl.when(jnp.logical_and((t + 1) % per == 0, t + 1 < blocks))
            def _():
                columns((t + 1) // per)

            @pl.when(t < steps - 1)
            def _():
                ahead(t)

        handed_over()
        receive(steps - 1)
        share(steps - 1)

        @pl.loop(0, steps)
        def _(t):
            gone = slots.at[t, pl.ds(0, devices - 1)]
            pltpu.make_async_copy(gone, gone, sum_send.at[t]).wait()
            if follow:
                gone = slots.at[t, pl.ds(0, len(follow))]
                pltpu.make_async_copy(gone, gone, scale_send.at[t]).wait()

    @pl.when(jnp.logical_not(on_plane))
    def _():
        @pl.loop(0, steps)
        def _(t):
            @pl.when(t == steps - 1)
            def _():
                handed_over()
            pltpu.make_async_copy(scales.at[t], scales.at[t], scale_sem.at[t]).wait()
            replay(t)


def local(dims, frames_y, traces, footprints, order, support):
    nx, ny, nz, nc = dims
    rows, span = frames_y.shape
    slab = traces.shape[0]
    neurons = footprints.shape[1]
    blocks = neurons // BLK
    steps = SWEEPS * blocks
    group = nz // ny
    devices = nx * ny * nc
    pixels = rows * lax.axis_size("pix")
    listed = -(-support.shape[1] // BLK)
    support = jnp.pad(support[0], (0, listed * BLK - support.shape[1]), constant_values=-1)
    dma = pltpu.SemaphoreType.DMA
    most = max(nx, ny)
    return pl.pallas_call(
        functools.partial(cnmf_kernel, dims, pixels),
        out_shape=jax.ShapeDtypeStruct((rows, neurons), F32),
        in_specs=[pl.BlockSpec(memory_space=pltpu.VMEM)] * 5,
        out_specs=pl.BlockSpec(memory_space=pltpu.VMEM),
        scratch_shapes=[
            pltpu.VMEM((neurons, neurons), BF16),
            pltpu.VMEM((blocks, 1, BLK), F32),
            pltpu.VMEM((rows, neurons), BF16),
            pltpu.VMEM((rows, neurons), BF16),
            pltpu.VMEM((ny, nx * nz, nc * slab, span), BF16),
            pltpu.VMEM((rows, ny * span), BF16),
            pltpu.VMEM((neurons, ny * span), BF16),
            pltpu.VMEM((rows, neurons), BF16),
            pltpu.VMEM((rows, neurons), BF16),
            pltpu.VMEM((2 * blocks, rows, BLK), F32),
            pltpu.VMEM((blocks, neurons, BLK), BF16),
            pltpu.VMEM((blocks, neurons, BLK), BF16),
            dma((2,)),
            dma,
            dma,
            dma((2, most - 1)),
            dma((2, most - 1, most)),
            dma((2, nx * ny)),
            dma,
            pltpu.VMEM((2 * blocks, group, rows, BLK), F32),
            pltpu.VMEM((steps, devices, 1, BLK), F32),
            pltpu.VMEM((steps, 1, BLK), F32),
            pltpu.VMEM((steps, 1, BLK), F32),
            pltpu.VMEM((group * rows, BLK), F32),
            pltpu.VMEM((group * rows, BLK), F32),
            pltpu.VMEM((group * rows, neurons), BF16),
            pltpu.VMEM((group * rows, neurons), BF16),
            pltpu.VMEM((rows, BLK), F32),
            pltpu.VMEM((rows, neurons), BF16),
            pltpu.VMEM((rows, neurons), BF16),
            dma((2 * blocks,)),
            dma,
            dma((steps,)),
            dma((steps,)),
            dma((steps,)),
            dma((steps,)),
        ],
        compiler_params=pltpu.CompilerParams(collective_id=1, has_side_effects=True),
        name="cnmf",
    )(frames_y, traces, footprints, order.reshape(blocks, 1, BLK), support.reshape(listed, 1, BLK))


def solution(mesh, dims=DIMS):
    placed = (P("pix", "frm"), P("pix", "frm"), P("pix", None), P(), P("pix", None))
    return jax.shard_map(
        functools.partial(local, dims), mesh=mesh, in_specs=placed,
        out_specs=P("pix", None), check_vma=False,
    )
```

```python
import functools

import jax
import jax.numpy as jnp
from jax import lax
from jax.experimental import pallas as pl
from jax.experimental.pallas import tpu as pltpu
from jax.sharding import PartitionSpec as P

BLK = 128
SWEEPS = 3
DIMS = (4, 4, 16, 2)
PLANES = 1
MESH = pl.DeviceIdType.MESH
F32, BF16 = jnp.float32, jnp.bfloat16


def ring_far(d, n):
    return min(d, n - d)


def plane_offsets(nx, ny, nc):
    every = [
        (dx, dy, dc)
        for dx in range(nx)
        for dy in range(ny)
        for dc in range(nc)
        if (dx, dy, dc) != (0, 0, 0)
    ]
    return sorted(every, key=lambda o: -(ring_far(o[0], nx) + ring_far(o[1], ny) + 0.1 * o[2]))


def split2(v):
    hi = v.astype(BF16)
    return hi, (v - hi.astype(F32)).astype(BF16)


def dot(a, b):
    return lax.dot_general(a, b, (((1,), (0,)), ((), ())), preferred_element_type=F32)


def dot3(ahi, alo, bhi, blo):
    return dot(ahi, bhi) + (dot(ahi, blo) + dot(alo, bhi))


def dot_t(a, b):
    return lax.dot_general(a, b, (((1,), (1,)), ((), ())), preferred_element_type=F32)


def cnmf_kernel(
    dims, pixels,
    frames, traces, footprints, order, support, out,
    onehot, kept, nhi, nlo, every, wide, ordered, fhi, flo, bases, mhi, mlo,
    own_sem, wide_sem, z_sem, first_sem, second_sem, core_sem, gather_send,
    planes, slots, sums, scales, acc, upd, chi, clo, oupd, ohi, olo,
    base_sem, base_send, sum_sem, sum_send, scale_sem, scale_send,
):
    nx, ny, nz, nc = dims
    group = nz // ny
    rows, neurons = out.shape
    blocks = neurons // BLK
    steps = SWEEPS * blocks
    devices = nx * ny * nc
    half = nz // 2
    slab, span = traces.shape
    pix, y = lax.axis_index("pix"), lax.axis_index("frm")
    x, z, c = pix // (nz * nc), (pix // nc) % nz, pix % nc
    me = (x * ny + y) * nc + c
    hop = nz // PLANES
    shift = (hop - 1) // 2
    on_plane = z % hop == 0
    follow = sorted((d for d in range(-shift, hop - shift) if d), key=lambda d: -abs(d))
    offsets = plane_offsets(nx, ny, nc)

    def place(ax, ay, az, ac):
        return ((ax * nz + az) * nc + ac, ay)

    def peer(offset):
        return place((x + offset[0]) % nx, (y + offset[1]) % ny, z, (c + offset[2]) % nc)

    barrier = pltpu.get_barrier_semaphore()

    def at_z(far):
        return place(x, y, (z + far) % nz, c)

    def at_x(far):
        return place((x + far) % nx, y, z, c)

    def at_y(far):
        return place(x, (y + far) % ny, z, c)

    other_core = place(x, y, z, (c + 1) % nc)
    near = (
        [at_z(far) for far in range(1, nz)]
        + [at_x(far) for far in range(1, nx)]
        + [at_y(far) for far in range(1, ny)]
        + [other_core] * (nc - 1)
    )
    apart = [o for o in offsets if (o[0] != 0) + (o[1] != 0) + (o[2] != 0) > 1]

    def greet(devices):
        for device in devices:
            pl.semaphore_signal(barrier, inc=1, device_id=device, device_id_type=MESH)

    greet(near)

    @pl.when(on_plane)
    def _():
        greet([peer(offset) for offset in apart])
        pl.semaphore_wait(barrier, len(near) + len(apart))

    @pl.when(jnp.logical_not(on_plane))
    def _():
        pl.semaphore_wait(barrier, len(near))

    mine = pl.ds(pl.multiple_of(c * slab, slab), slab)

    def remote(src, dst, sem, device):
        return pltpu.make_async_remote_copy(
            src_ref=src, dst_ref=dst, send_sem=gather_send, recv_sem=sem,
            device_id=device, device_id_type=MESH,
        )

    def arrived(ref, sem):
        pltpu.make_async_copy(ref, ref, sem).wait()

    sent = []

    def send(*copy):
        remote(*copy).start()
        sent.append(copy)

    home = every.at[y, x * nz + z, mine]
    own = pltpu.make_async_copy(traces, home, own_sem.at[0])
    own.start()
    for far in sorted(range(1, nz), key=lambda far: -ring_far(far, nz)):
        send(traces, home, z_sem, at_z(far))
    wide_part = wide.at[:, pl.ds(pl.multiple_of(y * span, span), span)]
    own_wide = pltpu.make_async_copy(frames, wide_part, own_sem.at[1])
    own_wide.start()
    for far in range(1, ny):
        send(frames, wide_part, wide_sem, at_y(far))

    row = lax.broadcasted_iota(jnp.int32, (BLK, BLK), 0)
    column = lax.broadcasted_iota(jnp.int32, (BLK, BLK), 1)
    ids = lax.broadcasted_iota(jnp.int32, (BLK, neurons), 1)

    def hits(line):
        upright = jnp.sum(jnp.where(row == column, line, 0), axis=1, keepdims=True)
        return jnp.where(upright == ids, 1.0, 0.0)

    for b in range(blocks):
        onehot[b * BLK:(b + 1) * BLK, :] = hits(order[b]).astype(BF16)
    listed = jnp.zeros((1, neurons), F32)
    for b in range(support.shape[0]):
        listed = jnp.maximum(listed, jnp.max(hits(support[b]), axis=0, keepdims=True))
    listed = dot_t(jnp.broadcast_to(listed, (8, neurons)).astype(BF16), onehot[...])
    for b in range(blocks):
        kept[b] = listed[:1, b * BLK:(b + 1) * BLK]
    old = footprints[...]
    hi, lo = split2(old)
    nhi[...] = hi
    nlo[...] = lo
    fhi[...] = dot_t(hi, onehot[...]).astype(BF16)
    flo[...] = dot_t(lo, onehot[...]).astype(BF16)

    own.wait()
    own_wide.wait()

    def low(ay, ax):
        return every.at[ay, pl.ds(ax * nz, half), mine]

    def high(ay, ax):
        return every.at[ay, pl.ds(ax * nz + half, half), mine]

    arrived(every.at[y, pl.ds(0, nz - 1), mine], z_sem)
    for far in range(1, nx):
        send(low(y, x), low(y, x), first_sem.at[0, far - 1], at_x(far))
    for far in range(1, ny):
        send(high(y, x), high(y, x), first_sem.at[1, far - 1], at_y(far))

    def finish(kind, part, ref):
        if nc > 1:
            send(ref, ref, core_sem.at[kind, part], other_core)

    def pass_on(kind, part, ref):
        peers, name = (ny, at_y) if kind == 0 else (nx, at_x)
        for far in range(1, peers):
            send(ref, ref, second_sem.at[kind, far - 1, part], name(far))
        finish(kind, part, ref)

    pass_on(0, 0, low(y, x))
    pass_on(1, 0, high(y, x))
    for far in range(1, max(nx, ny)):
        if far < nx:
            ref = low(y, (x + nx - far) % nx)
            arrived(ref, first_sem.at[0, far - 1])
            pass_on(0, far, ref)
        if far < ny:
            ref = high((y + ny - far) % ny, x)
            arrived(ref, first_sem.at[1, far - 1])
            pass_on(1, far, ref)
    for part in range(max(nx, ny)):
        for far in range(1, max(nx, ny)):
            if part < nx and far < ny:
                ref = low((y + ny - far) % ny, (x + nx - part) % nx)
                arrived(ref, second_sem.at[0, far - 1, part])
                finish(0, nx * far + part, ref)
            if part < ny and far < nx:
                ref = high((y + ny - part) % ny, (x + nx - far) % nx)
                arrived(ref, second_sem.at[1, far - 1, part])
                finish(1, ny * far + part, ref)
    if nc > 1:
        for part in range(nx * ny):
            arrived(low(0, 0), core_sem.at[0, part])
            arrived(high(0, 0), core_sem.at[1, part])
    arrived(wide.at[:, pl.ds(0, (ny - 1) * span)], wide_sem)

    def base_copy(i, plane):
        return pltpu.make_async_remote_copy(
            src_ref=bases.at[i], dst_ref=planes.at[i, z // ny],
            send_sem=base_send, recv_sem=base_sem.at[i],
            device_id=place(x, y, plane * hop, c), device_id_type=MESH,
        )

    gives = z % ny == y

    def lanes(b):
        return pl.ds(pl.multiple_of(b * BLK, BLK), BLK)

    def hand_over(i):
        for plane in range(PLANES):
            @pl.when(jnp.logical_and(gives, z != plane * hop))
            def _():
                base_copy(i, plane).start()

            @pl.when(jnp.logical_and(gives, z == plane * hop))
            def _():
                pltpu.make_async_copy(bases.at[i], planes.at[i, z // ny], base_sem.at[i]).start()

    def handed_over():
        for plane in range(PLANES):
            @pl.when(jnp.logical_and(gives, z != plane * hop))
            def _():
                for i in range(2 * blocks):
                    base_copy(i, plane).wait_send()

    width = min(256, neurons)
    per = width // BLK

    @pl.when(jnp.logical_not(on_plane))
    def _():
        gram = jnp.zeros((neurons, width), F32)
        for ay in range(ny):
            block = every[ay].reshape(neurons, span)
            some = dot(onehot[:width, :], block).astype(BF16)
            ordered[:width, ay * span:(ay + 1) * span] = some
            gram = gram + dot_t(block, some)
        some = ordered[:width, :]
        place_of = lax.broadcasted_iota(jnp.int32, (neurons, BLK), 0)
        cross = dot_t(wide[...], some)
        for b in range(per):
            part = slice(b * BLK, (b + 1) * BLK)
            same = place_of == order[b]
            diagonal = jnp.sum(jnp.where(same, gram[:, part], 0.0), axis=0, keepdims=True)
            hi, lo = split2(jnp.where(same, 0.0, gram[:, part]) / diagonal)
            start = jnp.where(kept[b] > 0.0, cross[:, part] / diagonal, -jnp.inf)
            if b == 0:
                ahi, alo = nhi[...], nlo[...]
            else:
                done = jnp.sum(onehot[:b * BLK, :].astype(F32), axis=0, keepdims=True)
                left = (1.0 - done).astype(BF16)
                ahi, alo = nhi[...] * left, nlo[...] * left
            bases[b] = start - dot3(ahi, alo, hi, lo)
            hand_over(b)

    @pl.loop(0, ny * span // width)
    def _(q):
        block = every[q * width // span, :, :, pl.ds(pl.multiple_of(q * width % span, width), width)]
        block = block.reshape(neurons, width)
        ordered[:, pl.ds(pl.multiple_of(q * width, width), width)] = dot(onehot[...], block).astype(BF16)

    def columns(q):
        some = ordered[pl.ds(pl.multiple_of(q * width, width), width), :]
        gram = dot_t(ordered[...], some)
        row = lax.broadcasted_iota(jnp.int32, gram.shape, 0)
        column = lax.broadcasted_iota(jnp.int32, gram.shape, 1) + q * width
        same = row == column
        diagonal = jnp.sum(jnp.where(same, gram, 0.0), axis=0, keepdims=True)
        hi, lo = split2(jnp.where(same, 0.0, gram) / diagonal)
        start = dot_t(wide[...], some) / diagonal
        for i in range(per):
            part = slice(i * BLK, (i + 1) * BLK)
            b = q * per + i
            mhi[b] = hi[:, part]
            mlo[b] = lo[:, part]
            bases[blocks + b] = jnp.where(kept[b] > 0.0, start[:, part], -jnp.inf)

            @pl.when(jnp.logical_or(on_plane, q > 0))
            def _():
                bases[b] = bases[blocks + b] - dot3(fhi[...], flo[...], mhi[b], mlo[b])
                hand_over(b)

            @pl.when(on_plane)
            def _():
                hand_over(blocks + b)

            fhi[:, lanes(b)] = jnp.zeros((rows, BLK), BF16)
            flo[:, lanes(b)] = jnp.zeros((rows, BLK), BF16)

    @pl.loop(0, jnp.where(on_plane, 1, blocks // per))
    def _(q):
        columns(q)

    for copy in sent:
        remote(*copy).wait_send()

    def base_index(t):
        return jnp.where(t < blocks, t, blocks + t % blocks)

    def sum_copy(t, offset):
        return pltpu.make_async_remote_copy(
            src_ref=sums.at[t], dst_ref=slots.at[t, me],
            send_sem=sum_send.at[t], recv_sem=sum_sem.at[t],
            device_id=peer(offset), device_id_type=MESH,
        )

    def scale_copy(t, far):
        return pltpu.make_async_remote_copy(
            src_ref=scales.at[t], dst_ref=scales.at[t],
            send_sem=scale_send.at[t], recv_sem=scale_sem.at[t],
            device_id=place(x, y, (z + far + nz) % nz, c), device_id_type=MESH,
        )

    oupd[...] = jnp.maximum(bases[0], 0.0)
    out[...] = jnp.zeros_like(out)
    ohi[...] = jnp.zeros_like(ohi)
    olo[...] = jnp.zeros_like(olo)

    def replay(t):
        b = t % blocks
        now = oupd[...] * scales[t]
        hi, lo = split2(now)
        ohi[:, lanes(b)] = hi
        olo[:, lanes(b)] = lo

        @pl.when(t >= steps - blocks)
        def _():
            rest = ((now - hi.astype(F32)) - lo.astype(F32)).astype(BF16)
            back = onehot[lanes(b), :]
            out[...] += (dot(hi, back) + dot(lo, back)) + dot(rest, back)

        @pl.when(t < steps - 1)
        def _():
            nxt = (t + 1) % blocks
            value = bases[base_index(t + 1)] - dot3(ohi[...], olo[...], mhi[nxt], mlo[nxt])
            oupd[...] = jnp.maximum(value, 0.0)

    def emit(t):
        new = jnp.maximum(acc[...], 0.0)
        upd[...] = new
        total = jnp.sum(new * new, axis=0, keepdims=True)
        sums[t] = total
        slots[t, me] = total
        for offset in offsets:
            sum_copy(t, offset).start()

    def prepare(t):
        @pl.when(t < 2 * blocks)
        def _():
            pltpu.make_async_copy(planes.at[t], planes.at[t], base_sem.at[t]).wait()
        return planes[base_index(t)].reshape(group * rows, BLK)

    def receive(t):
        waited = slots.at[t, pl.ds(0, devices - 1)]
        pltpu.make_async_copy(waited, waited, sum_sem.at[t]).wait()
        squares = jnp.sum(slots[t], axis=0)
        inverse = 1.0 / jnp.sqrt(squares / pixels + 1e-06)
        scales[t] = inverse
        return inverse

    def ahead(t):
        b = t % blocks
        nxt = (t + 1) % blocks
        chi[:, lanes(b)] = jnp.zeros((group * rows, BLK), BF16)
        clo[:, lanes(b)] = jnp.zeros((group * rows, BLK), BF16)
        base = prepare(t + 1)
        acc[...] = base - dot3(chi[...], clo[...], mhi[nxt], mlo[nxt])

    def share(t):
        for far in follow:
            scale_copy(t, far).start()
        replay(t)

    @pl.when(on_plane)
    def _():
        chi[...] = jnp.zeros_like(chi)
        clo[...] = jnp.zeros_like(clo)
        acc[...] = prepare(0)
        emit(0)
        ahead(0)

        @pl.loop(1, steps)
        def _(t):
            prev, b = (t - 1) % blocks, t % blocks
            now = upd[...] * receive(t - 1)
            hi, lo = split2(now)
            inner = pl.ds(pl.multiple_of(prev * BLK, BLK), BLK)
            acc[...] = acc[...] - dot3(hi, lo, mhi[b, inner], mlo[b, inner])
            emit(t)
            chi[:, lanes(prev)] = hi
            clo[:, lanes(prev)] = lo
            share(t - 1)

            @pl.when(jnp.logical_and((t + 1) % per == 0, t + 1 < blocks))
            def _():
                columns((t + 1) // per)

            @pl.when(t < steps - 1)
            def _():
                ahead(t)

        handed_over()
        receive(steps - 1)
        share(steps - 1)

        @pl.loop(0, steps)
        def _(t):
            gone = slots.at[t, pl.ds(0, devices - 1)]
            pltpu.make_async_copy(gone, gone, sum_send.at[t]).wait()
            if follow:
                gone = slots.at[t, pl.ds(0, len(follow))]
                pltpu.make_async_copy(gone, gone, scale_send.at[t]).wait()

    @pl.when(jnp.logical_not(on_plane))
    def _():
        @pl.loop(0, steps)
        def _(t):
            @pl.when(t == steps - 1)
            def _():
                handed_over()
            pltpu.make_async_copy(scales.at[t], scales.at[t], scale_sem.at[t]).wait()

            @pl.when(t < blocks)
            def _():
                hand_over(blocks + t)

            replay(t)


def local(dims, frames_y, traces, footprints, order, support):
    nx, ny, nz, nc = dims
    rows, span = frames_y.shape
    slab = traces.shape[0]
    neurons = footprints.shape[1]
    blocks = neurons // BLK
    steps = SWEEPS * blocks
    group = nz // ny
    devices = nx * ny * nc
    pixels = rows * lax.axis_size("pix")
    listed = -(-support.shape[1] // BLK)
    support = jnp.pad(support[0], (0, listed * BLK - support.shape[1]), constant_values=-1)
    dma = pltpu.SemaphoreType.DMA
    most = max(nx, ny)
    return pl.pallas_call(
        functools.partial(cnmf_kernel, dims, pixels),
        out_shape=jax.ShapeDtypeStruct((rows, neurons), F32),
        in_specs=[pl.BlockSpec(memory_space=pltpu.VMEM)] * 5,
        out_specs=pl.BlockSpec(memory_space=pltpu.VMEM),
        scratch_shapes=[
            pltpu.VMEM((neurons, neurons), BF16),
            pltpu.VMEM((blocks, 1, BLK), F32),
            pltpu.VMEM((rows, neurons), BF16),
            pltpu.VMEM((rows, neurons), BF16),
            pltpu.VMEM((ny, nx * nz, nc * slab, span), BF16),
            pltpu.VMEM((rows, ny * span), BF16),
            pltpu.VMEM((neurons, ny * span), BF16),
            pltpu.VMEM((rows, neurons), BF16),
            pltpu.VMEM((rows, neurons), BF16),
            pltpu.VMEM((2 * blocks, rows, BLK), F32),
            pltpu.VMEM((blocks, neurons, BLK), BF16),
            pltpu.VMEM((blocks, neurons, BLK), BF16),
            dma((2,)),
            dma,
            dma,
            dma((2, most - 1)),
            dma((2, most - 1, most)),
            dma((2, nx * ny)),
            dma,
            pltpu.VMEM((2 * blocks, group, rows, BLK), F32),
            pltpu.VMEM((steps, devices, 1, BLK), F32),
            pltpu.VMEM((steps, 1, BLK), F32),
            pltpu.VMEM((steps, 1, BLK), F32),
            pltpu.VMEM((group * rows, BLK), F32),
            pltpu.VMEM((group * rows, BLK), F32),
            pltpu.VMEM((group * rows, neurons), BF16),
            pltpu.VMEM((group * rows, neurons), BF16),
            pltpu.VMEM((rows, BLK), F32),
            pltpu.VMEM((rows, neurons), BF16),
            pltpu.VMEM((rows, neurons), BF16),
            dma((2 * blocks,)),
            dma,
            dma((steps,)),
            dma((steps,)),
            dma((steps,)),
            dma((steps,)),
        ],
        compiler_params=pltpu.CompilerParams(collective_id=1, has_side_effects=True),
        name="cnmf",
    )(frames_y, traces, footprints, order.reshape(blocks, 1, BLK), support.reshape(listed, 1, BLK))


def solution(mesh, dims=DIMS):
    placed = (P("pix", "frm"), P("pix", "frm"), P("pix", None), P(), P("pix", None))
    return jax.shard_map(
        functools.partial(local, dims), mesh=mesh, in_specs=placed,
        out_specs=P("pix", None), check_vma=False,
    )
```

```python
import functools

import jax
import jax.numpy as jnp
from jax import lax
from jax.experimental import pallas as pl
from jax.experimental.pallas import tpu as pltpu
from jax.sharding import PartitionSpec as P

BLK = 128
SWEEPS = 3
DIMS = (4, 4, 16, 2)
PLANES = 1
MESH = pl.DeviceIdType.MESH
F32, BF16 = jnp.float32, jnp.bfloat16


def ring_far(d, n):
    return min(d, n - d)


def plane_offsets(nx, ny, nc):
    every = [
        (dx, dy, dc)
        for dx in range(nx)
        for dy in range(ny)
        for dc in range(nc)
        if (dx, dy, dc) != (0, 0, 0)
    ]
    return sorted(every, key=lambda o: -(ring_far(o[0], nx) + ring_far(o[1], ny) + 0.1 * o[2]))


def split2(v):
    hi = v.astype(BF16)
    return hi, (v - hi.astype(F32)).astype(BF16)


def dot(a, b):
    return lax.dot_general(a, b, (((1,), (0,)), ((), ())), preferred_element_type=F32)


def dot3(ahi, alo, bhi, blo):
    return dot(ahi, bhi) + (dot(ahi, blo) + dot(alo, bhi))


def dot_t(a, b):
    return lax.dot_general(a, b, (((1,), (1,)), ((), ())), preferred_element_type=F32)


def cnmf_kernel(
    dims, pixels,
    frames, traces, footprints, order, support, out,
    onehot, kept, nhi, nlo, every, wide, ordered, fhi, flo, bases, mhi, mlo,
    own_sem, wide_sem, z_sem, first_sem, second_sem, core_sem, gather_send,
    planes, slots, sums, scales, acc, upd, chi, clo, oupd, ohi, olo,
    base_sem, base_send, sum_sem, sum_send, scale_sem, scale_send,
):
    nx, ny, nz, nc = dims
    group = nz // ny
    rows, neurons = out.shape
    blocks = neurons // BLK
    steps = SWEEPS * blocks
    devices = nx * ny * nc
    half = nz // 2
    slab, span = traces.shape
    pix, y = lax.axis_index("pix"), lax.axis_index("frm")
    x, z, c = pix // (nz * nc), (pix // nc) % nz, pix % nc
    me = (x * ny + y) * nc + c
    hop = nz // PLANES
    shift = (hop - 1) // 2
    on_plane = z % hop == 0
    follow = sorted((d for d in range(-shift, hop - shift) if d), key=lambda d: -abs(d))
    offsets = plane_offsets(nx, ny, nc)

    def place(ax, ay, az, ac):
        return ((ax * nz + az) * nc + ac, ay)

    def peer(offset):
        return place((x + offset[0]) % nx, (y + offset[1]) % ny, z, (c + offset[2]) % nc)

    barrier = pltpu.get_barrier_semaphore()

    def at_z(far):
        return place(x, y, (z + far) % nz, c)

    def at_x(far):
        return place((x + far) % nx, y, z, c)

    def at_y(far):
        return place(x, (y + far) % ny, z, c)

    other_core = place(x, y, z, (c + 1) % nc)
    near = (
        [at_z(far) for far in range(1, nz)]
        + [at_x(far) for far in range(1, nx)]
        + [at_y(far) for far in range(1, ny)]
        + [other_core] * (nc - 1)
    )
    apart = [o for o in offsets if (o[0] != 0) + (o[1] != 0) + (o[2] != 0) > 1]

    def greet(devices):
        for device in devices:
            pl.semaphore_signal(barrier, inc=1, device_id=device, device_id_type=MESH)

    greet(near)

    @pl.when(on_plane)
    def _():
        greet([peer(offset) for offset in apart])
        pl.semaphore_wait(barrier, len(near) + len(apart))

    @pl.when(jnp.logical_not(on_plane))
    def _():
        pl.semaphore_wait(barrier, len(near))

    mine = pl.ds(pl.multiple_of(c * slab, slab), slab)

    def remote(src, dst, sem, device):
        return pltpu.make_async_remote_copy(
            src_ref=src, dst_ref=dst, send_sem=gather_send, recv_sem=sem,
            device_id=device, device_id_type=MESH,
        )

    def arrived(ref, sem):
        pltpu.make_async_copy(ref, ref, sem).wait()

    sent = []

    def send(*copy):
        remote(*copy).start()
        sent.append(copy)

    home = every.at[y, x * nz + z, mine]
    own = pltpu.make_async_copy(traces, home, own_sem.at[0])
    own.start()
    for far in sorted(range(1, nz), key=lambda far: -ring_far(far, nz)):
        send(traces, home, z_sem, at_z(far))
    wide_part = wide.at[:, pl.ds(pl.multiple_of(y * span, span), span)]
    own_wide = pltpu.make_async_copy(frames, wide_part, own_sem.at[1])
    own_wide.start()
    for far in range(1, ny):
        send(frames, wide_part, wide_sem, at_y(far))

    row = lax.broadcasted_iota(jnp.int32, (BLK, BLK), 0)
    column = lax.broadcasted_iota(jnp.int32, (BLK, BLK), 1)
    ids = lax.broadcasted_iota(jnp.int32, (BLK, neurons), 1)

    def hits(line):
        upright = jnp.sum(jnp.where(row == column, line, 0), axis=1, keepdims=True)
        return jnp.where(upright == ids, 1.0, 0.0)

    for b in range(blocks):
        onehot[b * BLK:(b + 1) * BLK, :] = hits(order[b]).astype(BF16)
    listed = jnp.zeros((1, neurons), F32)
    for b in range(support.shape[0]):
        listed = jnp.maximum(listed, jnp.max(hits(support[b]), axis=0, keepdims=True))
    listed = dot_t(jnp.broadcast_to(listed, (8, neurons)).astype(BF16), onehot[...])
    for b in range(blocks):
        kept[b] = listed[:1, b * BLK:(b + 1) * BLK]
    old = footprints[...]
    hi, lo = split2(old)
    nhi[...] = hi
    nlo[...] = lo
    fhi[...] = dot_t(hi, onehot[...]).astype(BF16)
    flo[...] = dot_t(lo, onehot[...]).astype(BF16)

    own.wait()
    own_wide.wait()

    def low(ay, ax):
        return every.at[ay, pl.ds(ax * nz, half), mine]

    def high(ay, ax):
        return every.at[ay, pl.ds(ax * nz + half, half), mine]

    arrived(every.at[y, pl.ds(0, nz - 1), mine], z_sem)
    for far in range(1, nx):
        send(low(y, x), low(y, x), first_sem.at[0, far - 1], at_x(far))
    for far in range(1, ny):
        send(high(y, x), high(y, x), first_sem.at[1, far - 1], at_y(far))

    def finish(kind, part, ref):
        if nc > 1:
            send(ref, ref, core_sem.at[kind, part], other_core)

    def pass_on(kind, part, ref):
        peers, name = (ny, at_y) if kind == 0 else (nx, at_x)
        for far in range(1, peers):
            send(ref, ref, second_sem.at[kind, far - 1, part], name(far))
        finish(kind, part, ref)

    pass_on(0, 0, low(y, x))
    pass_on(1, 0, high(y, x))
    for far in range(1, max(nx, ny)):
        if far < nx:
            ref = low(y, (x + nx - far) % nx)
            arrived(ref, first_sem.at[0, far - 1])
            pass_on(0, far, ref)
        if far < ny:
            ref = high((y + ny - far) % ny, x)
            arrived(ref, first_sem.at[1, far - 1])
            pass_on(1, far, ref)
    for part in range(max(nx, ny)):
        for far in range(1, max(nx, ny)):
            if part < nx and far < ny:
                ref = low((y + ny - far) % ny, (x + nx - part) % nx)
                arrived(ref, second_sem.at[0, far - 1, part])
                finish(0, nx * far + part, ref)
            if part < ny and far < nx:
                ref = high((y + ny - part) % ny, (x + nx - far) % nx)
                arrived(ref, second_sem.at[1, far - 1, part])
                finish(1, ny * far + part, ref)
    if nc > 1:
        for part in range(nx * ny):
            arrived(low(0, 0), core_sem.at[0, part])
            arrived(high(0, 0), core_sem.at[1, part])
    arrived(wide.at[:, pl.ds(0, (ny - 1) * span)], wide_sem)

    def base_copy(i, plane):
        return pltpu.make_async_remote_copy(
            src_ref=bases.at[i], dst_ref=planes.at[i, z // ny],
            send_sem=base_send, recv_sem=base_sem.at[i],
            device_id=place(x, y, plane * hop, c), device_id_type=MESH,
        )

    gives = z % ny == y

    def lanes(b):
        return pl.ds(pl.multiple_of(b * BLK, BLK), BLK)

    def hand_over(i):
        for plane in range(PLANES):
            @pl.when(jnp.logical_and(gives, z != plane * hop))
            def _():
                base_copy(i, plane).start()

            @pl.when(jnp.logical_and(gives, z == plane * hop))
            def _():
                pltpu.make_async_copy(bases.at[i], planes.at[i, z // ny], base_sem.at[i]).start()

    def handed_over():
        for plane in range(PLANES):
            @pl.when(jnp.logical_and(gives, z != plane * hop))
            def _():
                for i in range(2 * blocks):
                    base_copy(i, plane).wait_send()

    width = min(256, neurons)
    per = width // BLK
    later = min(3, blocks // 2 - 1)

    @pl.when(jnp.logical_not(on_plane))
    def _():
        gram = jnp.zeros((neurons, width), F32)
        for ay in range(ny):
            block = every[ay].reshape(neurons, span)
            some = dot(onehot[:width, :], block).astype(BF16)
            ordered[:width, ay * span:(ay + 1) * span] = some
            gram = gram + dot_t(block, some)
        some = ordered[:width, :]
        place_of = lax.broadcasted_iota(jnp.int32, (neurons, BLK), 0)
        cross = dot_t(wide[...], some)
        for b in range(per):
            part = slice(b * BLK, (b + 1) * BLK)
            same = place_of == order[b]
            diagonal = jnp.sum(jnp.where(same, gram[:, part], 0.0), axis=0, keepdims=True)
            hi, lo = split2(jnp.where(same, 0.0, gram[:, part]) / diagonal)
            start = jnp.where(kept[b] > 0.0, cross[:, part] / diagonal, -jnp.inf)
            if b == 0:
                ahi, alo = nhi[...], nlo[...]
            else:
                done = jnp.sum(onehot[:b * BLK, :].astype(F32), axis=0, keepdims=True)
                left = (1.0 - done).astype(BF16)
                ahi, alo = nhi[...] * left, nlo[...] * left
            bases[b] = start - dot3(ahi, alo, hi, lo)
            if b == 0:
                hand_over(b)

    @pl.loop(0, ny * span // width)
    def _(q):
        block = every[q * width // span, :, :, pl.ds(pl.multiple_of(q * width % span, width), width)]
        block = block.reshape(neurons, width)
        ordered[:, pl.ds(pl.multiple_of(q * width, width), width)] = dot(onehot[...], block).astype(BF16)

    @pl.when(jnp.logical_not(on_plane))
    def _():
        for b in range(1, per):
            hand_over(b)

    def columns(q):
        some = ordered[pl.ds(pl.multiple_of(q * width, width), width), :]
        gram = dot_t(ordered[...], some)
        row = lax.broadcasted_iota(jnp.int32, gram.shape, 0)
        column = lax.broadcasted_iota(jnp.int32, gram.shape, 1) + q * width
        same = row == column
        diagonal = jnp.sum(jnp.where(same, gram, 0.0), axis=0, keepdims=True)
        hi, lo = split2(jnp.where(same, 0.0, gram) / diagonal)
        start = dot_t(wide[...], some) / diagonal
        for i in range(per):
            part = slice(i * BLK, (i + 1) * BLK)
            b = q * per + i
            mhi[b] = hi[:, part]
            mlo[b] = lo[:, part]
            bases[blocks + b] = jnp.where(kept[b] > 0.0, start[:, part], -jnp.inf)

            @pl.when(jnp.logical_or(on_plane, q > 0))
            def _():
                bases[b] = bases[blocks + b] - dot3(fhi[...], flo[...], mhi[b], mlo[b])
                hand_over(b)

            @pl.when(on_plane)
            def _():
                hand_over(blocks + b)

            fhi[:, lanes(b)] = jnp.zeros((rows, BLK), BF16)
            flo[:, lanes(b)] = jnp.zeros((rows, BLK), BF16)

    @pl.loop(0, jnp.where(on_plane, 1, blocks // per))
    def _(q):
        columns(q)

    for copy in sent:
        remote(*copy).wait_send()

    def base_index(t):
        return jnp.where(t < blocks, t, blocks + t % blocks)

    def sum_copy(t, offset):
        return pltpu.make_async_remote_copy(
            src_ref=sums.at[t], dst_ref=slots.at[t, me],
            send_sem=sum_send.at[t], recv_sem=sum_sem.at[t],
            device_id=peer(offset), device_id_type=MESH,
        )

    def scale_copy(t, far):
        return pltpu.make_async_remote_copy(
            src_ref=scales.at[t], dst_ref=scales.at[t],
            send_sem=scale_send.at[t], recv_sem=scale_sem.at[t],
            device_id=place(x, y, (z + far + nz) % nz, c), device_id_type=MESH,
        )

    oupd[...] = jnp.maximum(bases[0], 0.0)
    out[...] = jnp.zeros_like(out)
    ohi[...] = jnp.zeros_like(ohi)
    olo[...] = jnp.zeros_like(olo)

    def replay(t):
        b = t % blocks
        now = oupd[...] * scales[t]
        hi, lo = split2(now)
        ohi[:, lanes(b)] = hi
        olo[:, lanes(b)] = lo

        @pl.when(t >= steps - blocks)
        def _():
            rest = ((now - hi.astype(F32)) - lo.astype(F32)).astype(BF16)
            back = onehot[lanes(b), :]
            out[...] += (dot(hi, back) + dot(lo, back)) + dot(rest, back)

        @pl.when(t < steps - 1)
        def _():
            nxt = (t + 1) % blocks
            value = bases[base_index(t + 1)] - dot3(ohi[...], olo[...], mhi[nxt], mlo[nxt])
            oupd[...] = jnp.maximum(value, 0.0)

    def emit(t):
        new = jnp.maximum(acc[...], 0.0)
        upd[...] = new
        total = jnp.sum(new * new, axis=0, keepdims=True)
        sums[t] = total
        slots[t, me] = total
        for offset in offsets:
            sum_copy(t, offset).start()

    def prepare(t):
        @pl.when(t < 2 * blocks)
        def _():
            pltpu.make_async_copy(planes.at[t], planes.at[t], base_sem.at[t]).wait()
        return planes[base_index(t)].reshape(group * rows, BLK)

    def receive(t):
        waited = slots.at[t, pl.ds(0, devices - 1)]
        pltpu.make_async_copy(waited, waited, sum_sem.at[t]).wait()
        squares = jnp.sum(slots[t], axis=0)
        inverse = 1.0 / jnp.sqrt(squares / pixels + 1e-06)
        scales[t] = inverse
        return inverse

    def ahead(t):
        b = t % blocks
        nxt = (t + 1) % blocks
        chi[:, lanes(b)] = jnp.zeros((group * rows, BLK), BF16)
        clo[:, lanes(b)] = jnp.zeros((group * rows, BLK), BF16)
        base = prepare(t + 1)
        acc[...] = base - dot3(chi[...], clo[...], mhi[nxt], mlo[nxt])

    def share(t):
        for far in follow:
            scale_copy(t, far).start()
        replay(t)

    @pl.when(on_plane)
    def _():
        chi[...] = jnp.zeros_like(chi)
        clo[...] = jnp.zeros_like(clo)
        acc[...] = prepare(0)
        emit(0)
        ahead(0)

        @pl.loop(1, steps)
        def _(t):
            prev, b = (t - 1) % blocks, t % blocks
            now = upd[...] * receive(t - 1)
            hi, lo = split2(now)
            inner = pl.ds(pl.multiple_of(prev * BLK, BLK), BLK)
            acc[...] = acc[...] - dot3(hi, lo, mhi[b, inner], mlo[b, inner])
            emit(t)
            chi[:, lanes(prev)] = hi
            clo[:, lanes(prev)] = lo
            share(t - 1)

            @pl.when(jnp.logical_and((t + 1) % per == 0, t + 1 < blocks))
            def _():
                columns((t + 1) // per)

            @pl.when(t < steps - 1)
            def _():
                ahead(t)

        handed_over()
        receive(steps - 1)
        share(steps - 1)

        @pl.loop(0, steps)
        def _(t):
            gone = slots.at[t, pl.ds(0, devices - 1)]
            pltpu.make_async_copy(gone, gone, sum_send.at[t]).wait()
            if follow:
                gone = slots.at[t, pl.ds(0, len(follow))]
                pltpu.make_async_copy(gone, gone, scale_send.at[t]).wait()

    @pl.when(jnp.logical_not(on_plane))
    def _():
        @pl.loop(0, steps)
        def _(t):
            @pl.when(t == steps - 1)
            def _():
                handed_over()
            pltpu.make_async_copy(scales.at[t], scales.at[t], scale_sem.at[t]).wait()

            @pl.when(jnp.logical_and(t >= later, t < later + blocks))
            def _():
                hand_over(blocks + t - later)

            replay(t)


def local(dims, frames_y, traces, footprints, order, support):
    nx, ny, nz, nc = dims
    rows, span = frames_y.shape
    slab = traces.shape[0]
    neurons = footprints.shape[1]
    blocks = neurons // BLK
    steps = SWEEPS * blocks
    group = nz // ny
    devices = nx * ny * nc
    pixels = rows * lax.axis_size("pix")
    listed = -(-support.shape[1] // BLK)
    support = jnp.pad(support[0], (0, listed * BLK - support.shape[1]), constant_values=-1)
    dma = pltpu.SemaphoreType.DMA
    most = max(nx, ny)
    return pl.pallas_call(
        functools.partial(cnmf_kernel, dims, pixels),
        out_shape=jax.ShapeDtypeStruct((rows, neurons), F32),
        in_specs=[pl.BlockSpec(memory_space=pltpu.VMEM)] * 5,
        out_specs=pl.BlockSpec(memory_space=pltpu.VMEM),
        scratch_shapes=[
            pltpu.VMEM((neurons, neurons), BF16),
            pltpu.VMEM((blocks, 1, BLK), F32),
            pltpu.VMEM((rows, neurons), BF16),
            pltpu.VMEM((rows, neurons), BF16),
            pltpu.VMEM((ny, nx * nz, nc * slab, span), BF16),
            pltpu.VMEM((rows, ny * span), BF16),
            pltpu.VMEM((neurons, ny * span), BF16),
            pltpu.VMEM((rows, neurons), BF16),
            pltpu.VMEM((rows, neurons), BF16),
            pltpu.VMEM((2 * blocks, rows, BLK), F32),
            pltpu.VMEM((blocks, neurons, BLK), BF16),
            pltpu.VMEM((blocks, neurons, BLK), BF16),
            dma((2,)),
            dma,
            dma,
            dma((2, most - 1)),
            dma((2, most - 1, most)),
            dma((2, nx * ny)),
            dma,
            pltpu.VMEM((2 * blocks, group, rows, BLK), F32),
            pltpu.VMEM((steps, devices, 1, BLK), F32),
            pltpu.VMEM((steps, 1, BLK), F32),
            pltpu.VMEM((steps, 1, BLK), F32),
            pltpu.VMEM((group * rows, BLK), F32),
            pltpu.VMEM((group * rows, BLK), F32),
            pltpu.VMEM((group * rows, neurons), BF16),
            pltpu.VMEM((group * rows, neurons), BF16),
            pltpu.VMEM((rows, BLK), F32),
            pltpu.VMEM((rows, neurons), BF16),
            pltpu.VMEM((rows, neurons), BF16),
            dma((2 * blocks,)),
            dma,
            dma((steps,)),
            dma((steps,)),
            dma((steps,)),
            dma((steps,)),
        ],
        compiler_params=pltpu.CompilerParams(collective_id=1, has_side_effects=True),
        name="cnmf",
    )(frames_y, traces, footprints, order.reshape(blocks, 1, BLK), support.reshape(listed, 1, BLK))


def solution(mesh, dims=DIMS):
    placed = (P("pix", "frm"), P("pix", "frm"), P("pix", None), P(), P("pix", None))
    return jax.shard_map(
        functools.partial(local, dims), mesh=mesh, in_specs=placed,
        out_specs=P("pix", None), check_vma=False,
    )
```
